128 devices in a mesh: row: 16 (over y_lo, z, core), col: 8 (over x, y_hi).
Axes of the slice: x: 4, y: 4 (y_hi: 2, y_lo: 2; y = y_hi * 2 + y_lo), z: 4, core: 2. Of those that a mesh axis runs over, the one named last changes fastest.
Arguments:
- mode_basis: bfloat16 [16384, 4096], P('row'), may hold values from -0.0625 to 0.0625
- node_coords: float32 [3, 16384], P(None, 'row'), may hold values from -1 to 1
- quad_weights: float32 [16384], P('row'), may hold values from 0.3 to 3
- magnetization: bfloat16 [2, 4096, 128], P(None, 'col', 'row'), may hold values from -6 to 6
- decay_rates: float32 [4096], replicated, may hold values from 0.02 to 1.5
- directions: float32 [6, 3, 128], replicated, may hold values from -3 to 3
Outputs:
- final_magnet: bfloat16 [2, 4096, 128], P(None, 'col', 'row')
The draws below stay inside these ranges and needn't reach their ends.
All inputs are finite; a program needn't handle non-finite values.
Results may differ from the reference program's by a relative error of at most 0.03.
Values may be sent and summed in bfloat16 or wider, within the bound.
No kernel may reach another device: no remote copies, remote signals or barrier semaphores. Data moves between devices by JAX's collectives and lax.ppermute only.
A program may use at most 64 MiB of HBM per device.

```python
import math
import jax
import jax.numpy as jnp
from jax import lax

MODES = 4096
STEPS = 3
NODES = 16384
WAVEFORMS = 128
N_ROW = 16


def strengthened(drawn, own_key, source, target, blocks, factor):
    owner, partner = [(jnp.arange(drawn.shape[position]) // (drawn.shape[position] // blocks)).reshape([-1 if axis == position else 1 for axis in range(drawn.ndim)]) for position in (source, target)]
    chosen = jax.random.permutation(own_key, blocks)[partner]
    strong = (owner == chosen) | (owner == (partner + blocks // 2) % blocks)
    return jnp.where(strong, factor * drawn, drawn)


def shard_levels(rng, dims, cuts, low, largest):
    gain, own = 1.0, jax.random.fold_in(rng, 6)
    for position, parts in cuts:
        heights = jnp.exp(jax.random.uniform(jax.random.fold_in(own, position), (parts,), jnp.float32, low / len(cuts), largest / len(cuts)))
        gain = gain * jnp.repeat(heights, dims[position] // parts).reshape([-1 if axis == position else 1 for axis in range(len(dims))])
    return gain


def normal_values(key, extent, scale, bound, cuts=(), kind=jnp.bfloat16):
    entries = jax.random.normal(key, extent, jnp.float32) * scale
    if len(cuts) > 0:
        entries = shard_levels(key, extent, cuts, -0.22, 0.18) * entries
    return jnp.clip(entries, min=-bound, max=bound).astype(kind)


def bell_draw_with(own_key, shape, spread, limit, cuts, heavy, kind=jnp.bfloat16):
    array = spread * jax.random.normal(own_key, shape, jnp.float32)
    if cuts:
        array = array * shard_levels(own_key, shape, cuts, -0.22, 0.18)
    return jnp.clip(strengthened(array, jax.random.fold_in(own_key, 3), *heavy), -limit, limit).astype(kind)


def setup_inputs(seed: int = 0) -> dict:
    arg_keys = jax.random.split(jax.random.key(seed), 7)
    return {
        "mode_basis": bell_draw_with(arg_keys[0], (NODES, MODES), NODES ** -0.5, 0.0625, ((0, 16),), (0, 1, 16, 2.0)),
        "node_coords": jnp.clip(jax.random.uniform(arg_keys[1], (3, NODES), jnp.float32, -1.0, 1.0) * shard_levels(arg_keys[1], (3, NODES), ((1, 16),), -0.4, 0.0), -1.0, 1.0),
        "quad_weights": jnp.clip(jnp.exp(math.log(3.0) - 2.3025851 * jax.random.uniform(arg_keys[2], (NODES,), jnp.float32) ** shard_levels(arg_keys[2], (NODES,), ((0, 16),), -0.2, 0.2)), 0.3, 3.0),
        "magnetization": normal_values(arg_keys[3], (2, MODES, WAVEFORMS), 1.0, 6.0, ((1, 8), (2, 16))),
        "decay_rates": jnp.clip(jnp.exp(jax.random.uniform(arg_keys[4], (MODES,), jnp.float32, math.log(0.02), math.log(1.5))), 0.02, 1.5),
        "directions": normal_values(arg_keys[5], (2 * STEPS, 3, WAVEFORMS), 0.5, 3.0, (), jnp.float32),
    }


def reference(mode_basis, node_coords, quad_weights, magnetization, decay_rates, directions):
    moments = node_coords * quad_weights[None, :]
    slab_rows = NODES // N_ROW

    def add_slab(accum, slab_index):
        first_node = slab_index * slab_rows
        basis_slab = lax.dynamic_slice_in_dim(mode_basis, first_node, slab_rows, 0)
        moment_slab = lax.dynamic_slice_in_dim(moments, first_node, slab_rows, 1)
        pieces = []
        for axis_index in range(3):
            weighted = (basis_slab.astype(jnp.float32) * moment_slab[axis_index][:, None]).astype(jnp.bfloat16)
            partial_gram = lax.dot_general(basis_slab, weighted, (((0,), (0,)), ((), ())), preferred_element_type=jnp.float32)
            rounded = lax.optimization_barrier(partial_gram.astype(jnp.bfloat16))
            pieces.append(rounded.astype(jnp.float32))
        return accum + jnp.stack(pieces), None

    total_gram, _ = lax.scan(add_slab, jnp.zeros((3, MODES, MODES), jnp.float32), jnp.arange(N_ROW, dtype=jnp.int32))
    moment_gram = total_gram.astype(jnp.bfloat16)

    def apply_operator(field_now, weights_now, factor, keep_part):
        joined = jnp.concatenate([field_now[0], field_now[1]], axis=1)
        combined = jnp.zeros((MODES, 2 * WAVEFORMS), jnp.float32)
        for axis_index in range(3):
            scale_row = jnp.concatenate([weights_now[axis_index], weights_now[axis_index]])
            combined = combined + scale_row[None, :] * jnp.dot(moment_gram[axis_index], joined, preferred_element_type=jnp.float32)
        real_q = combined[:, :WAVEFORMS]
        imag_q = combined[:, WAVEFORMS:]
        diag_scale = (keep_part - factor * decay_rates)[:, None]
        field_float = field_now.astype(jnp.float32)
        new_real = factor * imag_q + diag_scale * field_float[0]
        new_imag = -factor * real_q + diag_scale * field_float[1]
        return jnp.stack([new_real, new_imag])

    field_now = magnetization
    for step_index in range(STEPS):
        half_field = apply_operator(field_now, directions[2 * step_index], 0.5, 1.0).astype(jnp.bfloat16)
        update = apply_operator(half_field, directions[2 * step_index + 1], 1.0, 0.0)
        field_now = (field_now.astype(jnp.float32) + update).astype(jnp.bfloat16)
    return field_now
```

```python
import jax
import jax.numpy as jnp
from jax import lax
from jax.sharding import PartitionSpec as P

STEPS = 3


def on_device(mode_basis, node_coords, quad_weights, magnetization, decay_rates, directions):
    row_count = lax.axis_size("row")
    col_count = lax.axis_size("col")
    row_index = lax.axis_index("row")
    col_index = lax.axis_index("col")
    mode_count = mode_basis.shape[1]
    node_local = mode_basis.shape[0]
    parts, col_width, own_waves = magnetization.shape
    lanes = mode_count // row_count
    columns = 2 * row_count
    f32, bf16 = jnp.float32, jnp.bfloat16

    mine = lax.dynamic_index_in_dim(
        directions.reshape(2 * STEPS, 3, row_count, own_waves), col_index, 3, keepdims=False
    )
    moments = node_coords * quad_weights[None, :]
    weights = jnp.sum(mine[:, :, :, None] * moments[None, :, None, :], axis=1)
    weights = jnp.concatenate([weights, weights], axis=1)

    def gather_rows(block):
        return lax.all_to_all(
            jnp.broadcast_to(block[None], (row_count,) + block.shape), "row", 0, 0
        )

    sent = jnp.transpose(magnetization, (2, 0, 1))
    own = lax.all_to_all(sent, "col", 0, 0)
    every = gather_rows(own)
    field_all = jnp.transpose(every, (2, 0, 1, 3)).reshape(columns, mode_count)

    def partial_sums(state, step):
        projected = lax.dot_general(
            state, mode_basis, (((1,), (1,)), ((), ())), preferred_element_type=f32
        )
        scaled = (projected * weights[step]).astype(bf16)
        return lax.dot_general(
            scaled, mode_basis, (((1,), (0,)), ((), ())), preferred_element_type=f32
        ).astype(bf16)

    def to_blocks(array):
        return jnp.transpose(array.reshape(columns, row_count, lanes), (1, 0, 2))

    def from_blocks(array):
        return jnp.transpose(array, (1, 0, 2)).reshape(columns, mode_count)

    def mixed(sums, factor):
        half = sums.shape[0] // 2
        return jnp.concatenate([factor * sums[half:], -factor * sums[:half]], axis=0)

    rates = lax.dynamic_slice_in_dim(decay_rates, row_index * lanes, lanes, 0)[None, :]
    field = lax.dynamic_slice_in_dim(field_all, row_index * lanes, lanes, 1)
    for step in range(STEPS):
        sums = lax.all_to_all(to_blocks(partial_sums(field_all, 2 * step)), "row", 0, 0)
        sums = jnp.sum(sums.astype(f32), axis=0)
        half = (mixed(sums, 0.5) + (1.0 - 0.5 * rates) * field.astype(f32)).astype(bf16)
        half_all = from_blocks(gather_rows(half))
        partial = partial_sums(half_all, 2 * step + 1)
        if step + 1 < STEPS:
            sums = lax.all_to_all(to_blocks(partial), "row", 0, 0)
            sums = jnp.sum(sums.astype(f32), axis=0)
            update = mixed(sums, 1.0) + (0.0 - 1.0 * rates) * half.astype(f32)
            field = (field.astype(f32) + update).astype(bf16)
            field_all = from_blocks(gather_rows(field))
        else:
            by_wave = jnp.transpose(partial.reshape(2, row_count, mode_count), (1, 0, 2))
            sums = lax.all_to_all(by_wave, "row", 0, 0)
            sums = jnp.sum(sums.astype(f32), axis=0)
            pick = lambda a: lax.dynamic_index_in_dim(
                a.reshape(2, row_count, mode_count), row_index, 1, keepdims=False
            ).astype(f32)
            update = mixed(sums, 1.0) + (0.0 - 1.0 * decay_rates[None, :]) * pick(half_all)
            own = (pick(field_all) + update).astype(bf16)
    sent = jnp.transpose(own.reshape(2, col_count, col_width), (1, 0, 2))
    return jnp.transpose(lax.all_to_all(sent, "col", 0, 0), (1, 2, 0))


def solution(mesh):
    return jax.shard_map(
        on_device,
        mesh=mesh,
        in_specs=(P("row", None), P(None, "row"), P("row"), P(None, "col", "row"), P(), P()),
        out_specs=P(None, "col", "row"),
        check_vma=False,
    )
```

```python
import jax
import jax.numpy as jnp
from jax import lax
from jax.sharding import PartitionSpec as P

STEPS = 3


def on_device(mode_basis, node_coords, quad_weights, magnetization, decay_rates, directions):
    row_count = lax.axis_size("row")
    col_count = lax.axis_size("col")
    row_index = lax.axis_index("row")
    col_index = lax.axis_index("col")
    mode_count = mode_basis.shape[1]
    node_local = mode_basis.shape[0]
    parts, col_width, own_waves = magnetization.shape
    lanes = mode_count // row_count
    columns = 2 * row_count
    f32, bf16 = jnp.float32, jnp.bfloat16

    mine = lax.dynamic_index_in_dim(
        directions.reshape(2 * STEPS, 3, row_count, own_waves), col_index, 3, keepdims=False
    )
    moments = node_coords * quad_weights[None, :]
    weights = jnp.sum(mine[:, :, :, None] * moments[None, :, None, :], axis=1)
    weights = jnp.concatenate([weights, weights], axis=1)

    def gather_rows(block):
        return lax.all_to_all(
            jnp.broadcast_to(block[None], (row_count,) + block.shape), "row", 0, 0
        )

    sent = jnp.transpose(magnetization, (2, 0, 1))
    own = lax.all_to_all(sent, "col", 0, 0)
    every = gather_rows(own)
    field_all = jnp.transpose(every, (2, 0, 1, 3)).reshape(columns, mode_count)

    def partial_sums(state, step):
        projected = lax.dot_general(
            state, mode_basis, (((1,), (1,)), ((), ())), preferred_element_type=f32
        )
        scaled = lax.optimization_barrier((projected * weights[step]).astype(bf16))
        return lax.dot_general(
            scaled, mode_basis, (((1,), (0,)), ((), ())), preferred_element_type=f32
        ).astype(bf16)

    def to_blocks(array):
        return jnp.transpose(array.reshape(columns, row_count, lanes), (1, 0, 2))

    def from_blocks(array):
        return jnp.transpose(array, (1, 0, 2)).reshape(columns, mode_count)

    def mixed(sums, factor):
        half = sums.shape[0] // 2
        return jnp.concatenate([factor * sums[half:], -factor * sums[:half]], axis=0)

    rates = lax.dynamic_slice_in_dim(decay_rates, row_index * lanes, lanes, 0)[None, :]
    field = lax.dynamic_slice_in_dim(field_all, row_index * lanes, lanes, 1)
    for step in range(STEPS):
        sums = lax.all_to_all(to_blocks(partial_sums(field_all, 2 * step)), "row", 0, 0)
        sums = jnp.sum(sums.astype(f32), axis=0)
        half = (mixed(sums, 0.5) + (1.0 - 0.5 * rates) * field.astype(f32)).astype(bf16)
        half_all = from_blocks(gather_rows(half))
        partial = partial_sums(half_all, 2 * step + 1)
        if step + 1 < STEPS:
            sums = lax.all_to_all(to_blocks(partial), "row", 0, 0)
            sums = jnp.sum(sums.astype(f32), axis=0)
            update = mixed(sums, 1.0) + (0.0 - 1.0 * rates) * half.astype(f32)
            field = (field.astype(f32) + update).astype(bf16)
            field_all = from_blocks(gather_rows(field))
        else:
            by_wave = jnp.transpose(partial.reshape(2, row_count, mode_count), (1, 0, 2))
            sums = lax.all_to_all(by_wave, "row", 0, 0)
            sums = jnp.sum(sums.astype(f32), axis=0)
            pick = lambda a: lax.dynamic_index_in_dim(
                a.reshape(2, row_count, mode_count), row_index, 1, keepdims=False
            ).astype(f32)
            update = mixed(sums, 1.0) + (0.0 - 1.0 * decay_rates[None, :]) * pick(half_all)
            own = (pick(field_all) + update).astype(bf16)
    sent = jnp.transpose(own.reshape(2, col_count, col_width), (1, 0, 2))
    return jnp.transpose(lax.all_to_all(sent, "col", 0, 0), (1, 2, 0))


def solution(mesh):
    return jax.shard_map(
        on_device,
        mesh=mesh,
        in_specs=(P("row", None), P(None, "row"), P("row"), P(None, "col", "row"), P(), P()),
        out_specs=P(None, "col", "row"),
        check_vma=False,
    )
```

```python
import jax
import jax.numpy as jnp
from jax import lax
from jax.sharding import PartitionSpec as P

STEPS = 3


def on_device(mode_basis, node_coords, quad_weights, magnetization, decay_rates, directions):
    row_count = lax.axis_size("row")
    col_count = lax.axis_size("col")
    row_index = lax.axis_index("row")
    col_index = lax.axis_index("col")
    core = row_index % 2
    mode_count = mode_basis.shape[1]
    parts, col_width, own_waves = magnetization.shape
    columns = 2 * row_count
    width = mode_count // 2
    f32, bf16 = jnp.float32, jnp.bfloat16

    def move(array, target):
        return lax.ppermute(array, "row", [(r, target(r)) for r in range(row_count)])

    def to_other_core(array):
        return move(array, lambda r: r ^ 1)

    def along_y(array):
        return move(array, lambda r: r ^ 8)

    def along_z(array, hops):
        return move(array, lambda r: (r & 9) | ((r + 2 * hops) & 6))

    mine = lax.dynamic_index_in_dim(
        directions.reshape(2 * STEPS, 3, row_count, own_waves), col_index, 3, keepdims=False
    )
    moments = node_coords * quad_weights[None, :]
    weights = jnp.sum(mine[:, :, :, None] * moments[None, :, None, :], axis=1)
    weights = jnp.concatenate([weights, weights], axis=1)

    def half_of(array, which, axis):
        return lax.dynamic_slice_in_dim(array, which * width, width, axis)

    basis_own = lax.optimization_barrier(half_of(mode_basis, core, 1))
    basis_other = lax.optimization_barrier(half_of(mode_basis, 1 - core, 1))
    rates = half_of(decay_rates, core, 0)[None, :]

    sent = jnp.transpose(magnetization, (2, 0, 1))
    sent = jnp.broadcast_to(sent[None], (row_count,) + sent.shape)
    sent = sent.reshape(row_count * col_count, parts, col_width)
    every = lax.all_to_all(sent, ("row", "col"), 0, 0)
    every = every.reshape(row_count, col_count, parts, col_width)
    every = jnp.transpose(every, (2, 0, 1, 3)).reshape(columns, mode_count)
    field = half_of(every, core, 1)
    field_other = half_of(every, 1 - core, 1)

    def scaled_nodes(own, other, step):
        nodes = lax.dot_general(
            own, basis_own, (((1,), (1,)), ((), ())), preferred_element_type=f32
        ) + lax.dot_general(
            other, basis_other, (((1,), (1,)), ((), ())), preferred_element_type=f32
        )
        return lax.optimization_barrier((nodes * weights[step]).astype(bf16))

    def back(nodes, basis):
        return lax.dot_general(
            nodes, basis, (((1,), (0,)), ((), ())), preferred_element_type=f32
        )

    def reduced(own, other, step):
        nodes = scaled_nodes(own, other, step)
        arrived = to_other_core(back(nodes, basis_other).astype(bf16))
        total = lax.optimization_barrier(back(nodes, basis_own)) + arrived.astype(f32)
        total = total + along_y(total.astype(bf16)).astype(f32)
        sent = total.astype(bf16)
        for hops in (1, 3, 2):
            total = total + along_z(sent, hops).astype(f32)
        return total

    def mixed(sums, factor):
        half = sums.shape[0] // 2
        return jnp.concatenate([factor * sums[half:], -factor * sums[:half]], axis=0)

    for step in range(STEPS):
        sums = reduced(field, field_other, 2 * step)
        half = (mixed(sums, 0.5) + (1.0 - 0.5 * rates) * field.astype(f32)).astype(bf16)
        half_other = to_other_core(half)
        if step + 1 < STEPS:
            sums = reduced(half, half_other, 2 * step + 1)
            update = mixed(sums, 1.0) + (0.0 - 1.0 * rates) * half.astype(f32)
            field = (field.astype(f32) + update).astype(bf16)
            field_other = to_other_core(field)

    nodes = scaled_nodes(half, half_other, 2 * STEPS - 1)
    local = field.astype(f32) + (0.0 - 1.0 * rates) * half.astype(f32)
    local = jnp.where(row_index < 2, local, 0.0)
    part_own = (mixed(back(nodes, basis_own), 1.0) + local).astype(bf16)
    part_other = mixed(back(nodes, basis_other), 1.0).astype(bf16)
    low = jnp.where(core == 0, part_own, part_other)
    high = jnp.where(core == 0, part_other, part_own)
    sent = jnp.concatenate([low, high], axis=1)
    sent = sent.reshape(parts, row_count, col_count, col_width)
    sent = jnp.transpose(sent, (1, 2, 0, 3)).reshape(row_count * col_count, parts, col_width)
    every = lax.all_to_all(sent, ("row", "col"), 0, 0)
    every = every.reshape(row_count, col_count, parts, col_width)
    final = jnp.sum(every.astype(f32), axis=0).astype(bf16)
    return jnp.transpose(final, (1, 2, 0))


def solution(mesh):
    return jax.shard_map(
        on_device,
        mesh=mesh,
        in_specs=(P("row", None), P(None, "row"), P("row"), P(None, "col", "row"), P(), P()),
        out_specs=P(None, "col", "row"),
        check_vma=False,
    )
```

```python
import jax
import jax.numpy as jnp
from jax import lax
from jax.sharding import PartitionSpec as P

STEPS = 3
CHUNKS = 2


def on_device(mode_basis, node_coords, quad_weights, magnetization, decay_rates, directions):
    row_count = lax.axis_size("row")
    col_count = lax.axis_size("col")
    row_index = lax.axis_index("row")
    col_index = lax.axis_index("col")
    core = row_index % 2
    mode_count = mode_basis.shape[1]
    node_local = mode_basis.shape[0]
    parts, col_width, own_waves = magnetization.shape
    columns = 2 * row_count
    width = mode_count // 2
    chunk = width // CHUNKS
    f32, bf16 = jnp.float32, jnp.bfloat16

    def move(array, target):
        return lax.ppermute(array, "row", [(r, target(r)) for r in range(row_count)])

    def to_other_core(array):
        return move(array, lambda r: r ^ 1)

    def along_y(array):
        return move(array, lambda r: r ^ 8)

    def along_z(array, hops):
        return move(array, lambda r: (r & 9) | ((r + 2 * hops) & 6))

    mine = lax.dynamic_index_in_dim(
        directions.reshape(2 * STEPS, 3, row_count, own_waves), col_index, 3, keepdims=False
    )
    moments = node_coords * quad_weights[None, :]
    weights = jnp.sum(mine[:, :, :, None] * moments[None, :, None, :], axis=1)

    sent = jnp.transpose(magnetization, (2, 0, 1))
    sent = jnp.broadcast_to(sent[None], (row_count,) + sent.shape)
    sent = sent.reshape(row_count * col_count, parts, col_width)
    every = lax.all_to_all(sent, ("row", "col"), 0, 0)
    every = every.reshape(row_count, col_count, parts, col_width)
    every = lax.optimization_barrier(
        jnp.transpose(every, (2, 0, 1, 3)).reshape(columns, mode_count)
    )

    def to_nodes(array, basis):
        return lax.dot_general(
            array, basis, (((1,), (1,)), ((), ())), preferred_element_type=f32
        )

    def to_modes(nodes, basis):
        return lax.dot_general(
            nodes, basis, (((1,), (0,)), ((), ())), preferred_element_type=f32
        )

    def turned(nodes, half_step):
        factor = 0.5 if half_step % 2 == 0 else 1.0
        scale = factor * weights[half_step]
        real, imag = nodes[:row_count], nodes[row_count:]
        rows = jnp.concatenate([scale * imag, -scale * real], axis=0)
        return lax.optimization_barrier(rows.astype(bf16))

    def over_chips(total):
        total = total + along_y(total.astype(bf16)).astype(f32)
        sent = total.astype(bf16)
        for hops in (1, 3, 2):
            total = total + along_z(sent, hops).astype(f32)
        return total

    def piece(array, which, k, axis):
        return lax.dynamic_slice_in_dim(array, which * width + k * chunk, chunk, axis)

    def pieces(array, which, axis):
        return [piece(array, which, k, axis) for k in range(CHUNKS)]

    def split(array):
        return [array[:, k * chunk : (k + 1) * chunk] for k in range(2 * CHUNKS)]

    nodes = turned(to_nodes(every, mode_basis), 0)
    partial = split(to_modes(nodes, mode_basis))
    low, high = partial[:CHUNKS], partial[CHUNKS:]
    arrived = [
        to_other_core(jnp.where(core == 0, b, a).astype(bf16)) for a, b in zip(low, high)
    ]
    totals = [
        over_chips(jnp.where(core == 0, a, b) + c.astype(f32))
        for a, b, c in zip(low, high, arrived)
    ]

    basis_own = [lax.optimization_barrier(b) for b in pieces(mode_basis, core, 1)]
    basis_other = [lax.optimization_barrier(b) for b in pieces(mode_basis, 1 - core, 1)]
    rates = [r[None, :] for r in pieces(decay_rates, core, 0)]
    field = pieces(every, core, 1)

    def reduced(own, half_step):
        other = [to_other_core(a) for a in own]
        nodes = None
        for array, basis in zip(own + other, basis_own + basis_other):
            term = lax.optimization_barrier(to_nodes(array, basis))
            nodes = term if nodes is None else nodes + term
        return turned(nodes, half_step)

    def summed(nodes):
        arrived = [to_other_core(to_modes(nodes, b).astype(bf16)) for b in basis_other]
        kept = [lax.optimization_barrier(to_modes(nodes, b)) for b in basis_own]
        return [over_chips(a + b.astype(f32)) for a, b in zip(kept, arrived)]

    for step in range(STEPS):
        if step > 0:
            totals = summed(reduced(field, 2 * step))
        half = [
            (s + (1.0 - 0.5 * r) * a.astype(f32)).astype(bf16)
            for s, r, a in zip(totals, rates, field)
        ]
        nodes = reduced(half, 2 * step + 1)
        if step + 1 < STEPS:
            totals = summed(nodes)
            field = [
                (a.astype(f32) + (s + (0.0 - 1.0 * r) * h.astype(f32))).astype(bf16)
                for s, r, a, h in zip(totals, rates, field, half)
            ]

    part_own, part_other = [], []
    for a, h, r, own, other in zip(field, half, rates, basis_own, basis_other):
        local = a.astype(f32) + (0.0 - 1.0 * r) * h.astype(f32)
        local = jnp.where(row_index < 2, local, 0.0)
        part_own.append((to_modes(nodes, own) + local).astype(bf16))
        part_other.append(to_modes(nodes, other).astype(bf16))
    low = [jnp.where(core == 0, a, b) for a, b in zip(part_own, part_other)]
    high = [jnp.where(core == 0, b, a) for a, b in zip(part_own, part_other)]
    sent = jnp.concatenate(low + high, axis=1)
    sent = sent.reshape(parts, row_count, col_count, col_width)
    sent = jnp.transpose(sent, (1, 2, 0, 3)).reshape(row_count * col_count, parts, col_width)
    every = lax.all_to_all(sent, ("row", "col"), 0, 0)
    every = every.reshape(row_count, col_count, parts, col_width)
    final = jnp.sum(every.astype(f32), axis=0).astype(bf16)
    return jnp.transpose(final, (1, 2, 0))


def solution(mesh):
    return jax.shard_map(
        on_device,
        mesh=mesh,
        in_specs=(P("row", None), P(None, "row"), P("row"), P(None, "col", "row"), P(), P()),
        out_specs=P(None, "col", "row"),
        check_vma=False,
    )
```

```python
import jax
import jax.numpy as jnp
from jax import lax
from jax.sharding import PartitionSpec as P

STEPS = 3


def on_device(mode_basis, node_coords, quad_weights, magnetization, decay_rates, directions):
    row_count = lax.axis_size("row")
    col_count = lax.axis_size("col")
    row_index = lax.axis_index("row")
    col_index = lax.axis_index("col")
    core = row_index % 2
    mode_count = mode_basis.shape[1]
    node_local = mode_basis.shape[0]
    parts, col_width, own_waves = magnetization.shape
    columns = 2 * row_count
    width = mode_count // 2
    f32, bf16 = jnp.float32, jnp.bfloat16

    def move(array, target):
        return lax.ppermute(array, "row", [(r, target(r)) for r in range(row_count)])

    def to_other_core(array):
        return move(array, lambda r: r ^ 1)

    def y_of(r):
        return r ^ 8

    def z_of(r, hops):
        return (r & 9) | ((r + 2 * hops) & 6)

    def exchanged(array, z_core):
        sent = array.astype(bf16)
        pairs = [(r, z_of(r, 1) if r % 2 == z_core else y_of(r)) for r in range(row_count)]
        total = array + lax.ppermute(sent, "row", pairs).astype(f32)
        for hops in (3, 2):
            pairs = [(r, z_of(r, hops)) for r in range(row_count) if r % 2 == z_core]
            total = total + lax.ppermute(sent, "row", pairs).astype(f32)
        return total

    def over_chips(array):
        return exchanged(exchanged(array, 1), 0)

    mine = lax.dynamic_index_in_dim(
        directions.reshape(2 * STEPS, 3, row_count, own_waves), col_index, 3, keepdims=False
    )
    moments = node_coords * quad_weights[None, :]
    weights = jnp.sum(mine[:, :, :, None] * moments[None, :, None, :], axis=1)

    sent = jnp.transpose(magnetization, (2, 0, 1))
    sent = jnp.broadcast_to(sent[None], (row_count,) + sent.shape)
    sent = sent.reshape(row_count * col_count, parts, col_width)
    every = lax.all_to_all(sent, ("row", "col"), 0, 0)
    every = every.reshape(row_count, col_count, parts, col_width)
    every = lax.optimization_barrier(
        jnp.transpose(every, (2, 0, 1, 3)).reshape(columns, mode_count)
    )

    def to_nodes(array, basis):
        return lax.dot_general(
            array, basis, (((1,), (1,)), ((), ())), preferred_element_type=f32
        )

    def to_modes(nodes, basis):
        return lax.dot_general(
            nodes, basis, (((1,), (0,)), ((), ())), preferred_element_type=f32
        )

    def turned(nodes, half_step):
        factor = 0.5 if half_step % 2 == 0 else 1.0
        scale = factor * weights[half_step]
        real, imag = nodes[:row_count], nodes[row_count:]
        rows = jnp.concatenate([scale * imag, -scale * real], axis=0)
        return lax.optimization_barrier(rows.astype(bf16))

    def half_of(array, which, axis):
        return lax.dynamic_slice_in_dim(array, which * width, width, axis)

    basis_own, rest = lax.optimization_barrier((half_of(mode_basis, core, 1), mode_basis))
    basis_other = lax.optimization_barrier(half_of(rest, 1 - core, 1))
    rates = half_of(decay_rates, core, 0)[None, :]
    field = half_of(every, core, 1)
    field_other = half_of(every, 1 - core, 1)

    def weighted(own, other, half_step):
        kept = lax.optimization_barrier(to_nodes(own, basis_own))
        return turned(kept + to_nodes(other, basis_other), half_step)

    def summed(nodes):
        arrived = to_other_core(to_modes(nodes, basis_other).astype(bf16))
        kept = lax.optimization_barrier(to_modes(nodes, basis_own))
        return over_chips(kept + arrived.astype(f32))

    for step in range(STEPS):
        sums = summed(weighted(field, field_other, 2 * step))
        half = (sums + (1.0 - 0.5 * rates) * field.astype(f32)).astype(bf16)
        nodes = weighted(half, to_other_core(half), 2 * step + 1)
        if step + 1 < STEPS:
            update = summed(nodes) + (0.0 - 1.0 * rates) * half.astype(f32)
            field = (field.astype(f32) + update).astype(bf16)
            field_other = to_other_core(field)

    local = field.astype(f32) + (0.0 - 1.0 * rates) * half.astype(f32)
    local = jnp.where(row_index < 2, local, 0.0)
    part_own = (to_modes(nodes, basis_own) + local).astype(bf16)
    part_other = to_modes(nodes, basis_other).astype(bf16)
    low = jnp.where(core == 0, part_own, part_other)
    high = jnp.where(core == 0, part_other, part_own)
    sent = jnp.concatenate([low, high], axis=1)
    sent = sent.reshape(parts, row_count, col_count, col_width)
    sent = jnp.transpose(sent, (1, 2, 0, 3)).reshape(row_count * col_count, parts, col_width)
    every = lax.all_to_all(sent, ("row", "col"), 0, 0)
    every = every.reshape(row_count, col_count, parts, col_width)
    final = jnp.sum(every.astype(f32), axis=0).astype(bf16)
    return jnp.transpose(final, (1, 2, 0))


def solution(mesh):
    return jax.shard_map(
        on_device,
        mesh=mesh,
        in_specs=(P("row", None), P(None, "row"), P("row"), P(None, "col", "row"), P(), P()),
        out_specs=P(None, "col", "row"),
        check_vma=False,
    )
```

```python
import jax
import jax.numpy as jnp
from jax import lax
from jax.sharding import PartitionSpec as P

STEPS = 3


def on_device(mode_basis, node_coords, quad_weights, magnetization, decay_rates, directions):
    row_count = lax.axis_size("row")
    col_count = lax.axis_size("col")
    row_index = lax.axis_index("row")
    col_index = lax.axis_index("col")
    core = row_index % 2
    mode_count = mode_basis.shape[1]
    node_local = mode_basis.shape[0]
    parts, col_width, own_waves = magnetization.shape
    columns = 2 * row_count
    width = mode_count // 2
    f32, bf16 = jnp.float32, jnp.bfloat16

    def move(array, target):
        return lax.ppermute(array, "row", [(r, target(r)) for r in range(row_count)])

    def to_other_core(array):
        return move(array, lambda r: r ^ 1)

    rounds = ((8, 2), (2, 6), (6, 8))

    def over_chips(total):
        for bits in rounds:
            total = total + move(total.astype(bf16), lambda r: r ^ bits[r % 2]).astype(f32)
        return total

    mine = lax.dynamic_index_in_dim(
        directions.reshape(2 * STEPS, 3, row_count, own_waves), col_index, 3, keepdims=False
    )
    moments = node_coords * quad_weights[None, :]
    weights = jnp.sum(mine[:, :, :, None] * moments[None, :, None, :], axis=1)

    sent = jnp.transpose(magnetization, (2, 0, 1))
    sent = jnp.broadcast_to(sent[None], (row_count,) + sent.shape)
    sent = sent.reshape(row_count * col_count, parts, col_width)
    every = lax.all_to_all(sent, ("row", "col"), 0, 0)
    every = every.reshape(row_count, col_count, parts, col_width)
    every = lax.optimization_barrier(
        jnp.transpose(every, (2, 0, 1, 3)).reshape(columns, mode_count)
    )

    def to_nodes(array, basis):
        return lax.dot_general(
            array, basis, (((1,), (1,)), ((), ())), preferred_element_type=f32
        )

    def to_modes(nodes, basis):
        return lax.dot_general(
            nodes, basis, (((1,), (0,)), ((), ())), preferred_element_type=f32
        )

    def turned(nodes, half_step):
        factor = 0.5 if half_step % 2 == 0 else 1.0
        scale = factor * weights[half_step]
        real, imag = nodes[:row_count], nodes[row_count:]
        rows = jnp.concatenate([scale * imag, -scale * real], axis=0)
        return lax.optimization_barrier(rows.astype(bf16))

    def half_of(array, which, axis):
        return lax.dynamic_slice_in_dim(array, which * width, width, axis)

    basis_own = half_of(mode_basis, core, 1)
    basis_other = half_of(mode_basis, 1 - core, 1)
    rates = half_of(decay_rates, core, 0)[None, :]
    field = half_of(every, core, 1)
    field_other = half_of(every, 1 - core, 1)

    def weighted(own, other, half_step):
        kept = lax.optimization_barrier(to_nodes(own, basis_own))
        return turned(kept + to_nodes(other, basis_other), half_step)

    def summed(nodes):
        arrived = to_other_core(to_modes(nodes, basis_other).astype(bf16))
        kept = lax.optimization_barrier(to_modes(nodes, basis_own))
        return over_chips(kept + arrived.astype(f32))

    for step in range(STEPS):
        sums = summed(weighted(field, field_other, 2 * step))
        half = (sums + (1.0 - 0.5 * rates) * field.astype(f32)).astype(bf16)
        nodes = weighted(half, to_other_core(half), 2 * step + 1)
        if step + 1 < STEPS:
            update = summed(nodes) + (0.0 - 1.0 * rates) * half.astype(f32)
            field = (field.astype(f32) + update).astype(bf16)
            field_other = to_other_core(field)

    local = field.astype(f32) + (0.0 - 1.0 * rates) * half.astype(f32)
    local = jnp.where(row_index < 2, local, 0.0)
    part_own = (to_modes(nodes, basis_own) + local).astype(bf16)
    part_other = to_modes(nodes, basis_other).astype(bf16)
    low = jnp.where(core == 0, part_own, part_other)
    high = jnp.where(core == 0, part_other, part_own)
    sent = jnp.concatenate([low, high], axis=1)
    sent = sent.reshape(parts, row_count, col_count, col_width)
    sent = jnp.transpose(sent, (1, 2, 0, 3)).reshape(row_count * col_count, parts, col_width)
    every = lax.all_to_all(sent, ("row", "col"), 0, 0)
    every = every.reshape(row_count, col_count, parts, col_width)
    final = jnp.sum(every.astype(f32), axis=0).astype(bf16)
    return jnp.transpose(final, (1, 2, 0))


def solution(mesh):
    return jax.shard_map(
        on_device,
        mesh=mesh,
        in_specs=(P("row", None), P(None, "row"), P("row"), P(None, "col", "row"), P(), P()),
        out_specs=P(None, "col", "row"),
        check_vma=False,
    )
```

```python
import jax
import jax.numpy as jnp
from jax import lax
from jax.sharding import PartitionSpec as P

STEPS = 3


def on_device(mode_basis, node_coords, quad_weights, magnetization, decay_rates, directions):
    row_count = lax.axis_size("row")
    col_count = lax.axis_size("col")
    row_index = lax.axis_index("row")
    col_index = lax.axis_index("col")
    core = row_index % 2
    mode_count = mode_basis.shape[1]
    node_local = mode_basis.shape[0]
    parts, col_width, own_waves = magnetization.shape
    columns = 2 * row_count
    width = mode_count // 2
    f32, bf16 = jnp.float32, jnp.bfloat16

    def move(array, target):
        return lax.ppermute(array, "row", [(r, target(r)) for r in range(row_count)])

    def to_other_core(array):
        return move(array, lambda r: r ^ 1)

    def along_y(array):
        return move(array, lambda r: r ^ 8)

    def along_z(array, hops):
        return move(array, lambda r: (r & 9) | ((r + 2 * hops) & 6))

    def over_chips(total):
        total = total + along_y(total.astype(bf16)).astype(f32)
        sent = total.astype(bf16)
        for hops in (1, 3, 2):
            total = total + along_z(sent, hops).astype(f32)
        return total

    mine = lax.dynamic_index_in_dim(
        directions.reshape(2 * STEPS, 3, row_count, own_waves), col_index, 3, keepdims=False
    )
    pairs = row_count // 2
    mine = jnp.swapaxes(mine.reshape(2 * STEPS, 3, pairs, 2), 2, 3)
    mine = mine.reshape(2 * STEPS, 3, row_count)
    moments = node_coords * quad_weights[None, :]
    weights = jnp.sum(mine[:, :, :, None] * moments[None, :, None, :], axis=1)

    device = [r * col_count + c for r in range(row_count) for c in range(col_count)]
    same_core = [[d for d in device if (d // col_count) % 2 == k] for k in (0, 1)]

    def all_places(array):
        array = array.reshape(pairs * col_count, parts, col_width)
        array = lax.all_to_all(array, ("row", "col"), 0, 0, axis_index_groups=same_core)
        return array.reshape(pairs, col_count, parts, col_width)

    sent = jnp.transpose(magnetization, (2, 0, 1))
    sent = jnp.broadcast_to(sent[None], (pairs,) + sent.shape)
    own_at = (core * width).astype(jnp.uint32)
    other_at = (width - core * width).astype(jnp.uint32)
    first_core, first_chip = core == 0, row_index < 2
    own_at, other_at = lax.optimization_barrier((own_at, other_at))

    def half_of(array, which, axis):
        return lax.dynamic_slice_in_dim(array, which, width, axis)

    rates = jnp.stack([half_of(decay_rates, own_at, 0), half_of(decay_rates, other_at, 0)])
    sent, weights, rates, first_core, first_chip = lax.optimization_barrier(
        (sent, weights, rates, first_core, first_chip)
    )
    rates = rates[:1]

    def by_parity(own, other):
        return jnp.where(first_core, own, other), jnp.where(first_core, other, own)

    every = jnp.transpose(all_places(sent), (2, 0, 1, 3)).reshape(parts, pairs, mode_count)
    every = jnp.stack(by_parity(every, to_other_core(every)), axis=1)
    every = lax.optimization_barrier(every.reshape(columns, mode_count))

    def to_nodes(array, basis):
        return lax.dot_general(
            array, basis, (((1,), (1,)), ((), ())), preferred_element_type=f32
        )

    def to_modes(nodes, basis):
        return lax.dot_general(
            nodes, basis, (((1,), (0,)), ((), ())), preferred_element_type=f32
        )

    def turned(nodes, half_step):
        factor = 0.5 if half_step % 2 == 0 else 1.0
        scale = factor * weights[half_step]
        real, imag = nodes[:row_count], nodes[row_count:]
        rows = jnp.concatenate([scale * imag, -scale * real], axis=0)
        return lax.optimization_barrier(rows.astype(bf16))

    basis_own = half_of(mode_basis, own_at, 1)
    basis_other = half_of(mode_basis, other_at, 1)
    field = half_of(every, own_at, 1)
    field_other = half_of(every, other_at, 1)

    def weighted(own, other, half_step):
        kept = lax.optimization_barrier(to_nodes(own, basis_own))
        return turned(kept + to_nodes(other, basis_other), half_step)

    def summed(nodes):
        arrived = to_other_core(to_modes(nodes, basis_other).astype(bf16))
        kept = lax.optimization_barrier(to_modes(nodes, basis_own))
        return over_chips(kept + arrived.astype(f32))

    for step in range(STEPS):
        sums = summed(weighted(field, field_other, 2 * step))
        half = (sums + (1.0 - 0.5 * rates) * field.astype(f32)).astype(bf16)
        nodes = weighted(half, to_other_core(half), 2 * step + 1)
        if step + 1 < STEPS:
            update = summed(nodes) + (0.0 - 1.0 * rates) * half.astype(f32)
            field = (field.astype(f32) + update).astype(bf16)
            field_other = to_other_core(field)

    local = field.astype(f32) + (0.0 - 1.0 * rates) * half.astype(f32)
    local = jnp.where(first_chip, local, 0.0)
    low = jnp.where(first_core, local, 0.0)
    high = jnp.where(first_core, 0.0, local)
    partial = to_modes(nodes, mode_basis) + jnp.concatenate([low, high], axis=1)
    partial = partial.astype(bf16).reshape(parts, 2, pairs, mode_count)
    kept, sent = by_parity(partial[:, 0], partial[:, 1])
    sent = (kept.astype(f32) + to_other_core(sent).astype(f32)).astype(bf16)
    sent = jnp.transpose(sent.reshape(parts, pairs, col_count, col_width), (1, 2, 0, 3))
    final = jnp.sum(all_places(sent).astype(f32), axis=0).astype(bf16)
    return jnp.transpose(final, (1, 2, 0))


def solution(mesh):
    return jax.shard_map(
        on_device,
        mesh=mesh,
        in_specs=(P("row", None), P(None, "row"), P("row"), P(None, "col", "row"), P(), P()),
        out_specs=P(None, "col", "row"),
        check_vma=False,
    )
```

```python
import jax
import jax.numpy as jnp
from jax import lax
from jax.sharding import PartitionSpec as P

STEPS = 3


def on_device(mode_basis, node_coords, quad_weights, magnetization, decay_rates, directions):
    row_count = lax.axis_size("row")
    col_count = lax.axis_size("col")
    row_index = lax.axis_index("row")
    col_index = lax.axis_index("col")
    core = row_index % 2
    mode_count = mode_basis.shape[1]
    node_local = mode_basis.shape[0]
    parts, col_width, own_waves = magnetization.shape
    columns = 2 * row_count
    width = mode_count // 2
    f32, bf16 = jnp.float32, jnp.bfloat16

    def move(array, target):
        return lax.ppermute(array, "row", [(r, target(r)) for r in range(row_count)])

    def to_other_core(array):
        return move(array, lambda r: r ^ 1)

    def along_y(array):
        return move(array, lambda r: r ^ 8)

    def along_z(array, hops):
        return move(array, lambda r: (r & 9) | ((r + 2 * hops) & 6))

    def over_chips(total):
        total = total + along_y(total.astype(bf16)).astype(f32)
        sent = total.astype(bf16)
        for hops in (1, 3, 2):
            total = total + along_z(sent, hops).astype(f32)
        return total

    mine = lax.dynamic_index_in_dim(
        directions.reshape(2 * STEPS, 3, row_count, own_waves), col_index, 3, keepdims=False
    )
    moments = node_coords * quad_weights[None, :]
    weights = jnp.sum(mine[:, :, :, None] * moments[None, :, None, :], axis=1)

    sent = jnp.transpose(magnetization, (2, 0, 1))
    sent = jnp.broadcast_to(sent[None], (row_count,) + sent.shape)
    sent = sent.reshape(row_count * col_count, parts, col_width)
    first_core, first_chip = core == 0, row_index < 2

    def half_of(array, which, axis):
        return lax.dynamic_slice_in_dim(array, which * width, width, axis)

    rates = jnp.stack([half_of(decay_rates, core, 0), half_of(decay_rates, 1 - core, 0)])
    sent, rates, first_core, first_chip = lax.optimization_barrier(
        (sent, rates, first_core, first_chip)
    )
    rates = rates[:1]
    every = lax.all_to_all(sent, ("row", "col"), 0, 0)
    every = every.reshape(row_count, col_count, parts, col_width)
    every = lax.optimization_barrier(
        jnp.transpose(every, (2, 0, 1, 3)).reshape(columns, mode_count)
    )

    def to_nodes(array, basis):
        return lax.dot_general(
            array, basis, (((1,), (1,)), ((), ())), preferred_element_type=f32
        )

    def to_modes(nodes, basis):
        return lax.dot_general(
            nodes, basis, (((1,), (0,)), ((), ())), preferred_element_type=f32
        )

    def turned(nodes, half_step):
        factor = 0.5 if half_step % 2 == 0 else 1.0
        scale = factor * weights[half_step]
        real, imag = nodes[:row_count], nodes[row_count:]
        rows = jnp.concatenate([scale * imag, -scale * real], axis=0)
        return lax.optimization_barrier(rows.astype(bf16))

    basis_own = half_of(mode_basis, core, 1)
    basis_other = half_of(mode_basis, 1 - core, 1)
    field = half_of(every, core, 1)
    field_other = half_of(every, 1 - core, 1)

    def weighted(own, other, half_step):
        kept = lax.optimization_barrier(to_nodes(own, basis_own))
        return turned(kept + to_nodes(other, basis_other), half_step)

    def summed(nodes):
        arrived = to_other_core(to_modes(nodes, basis_other).astype(bf16))
        kept = lax.optimization_barrier(to_modes(nodes, basis_own))
        return over_chips(kept + arrived.astype(f32))

    for step in range(STEPS):
        sums = summed(weighted(field, field_other, 2 * step))
        half = (sums + (1.0 - 0.5 * rates) * field.astype(f32)).astype(bf16)
        nodes = weighted(half, to_other_core(half), 2 * step + 1)
        if step + 1 < STEPS:
            update = summed(nodes) + (0.0 - 1.0 * rates) * half.astype(f32)
            field = (field.astype(f32) + update).astype(bf16)
            field_other = to_other_core(field)

    local = field.astype(f32) + (0.0 - 1.0 * rates) * half.astype(f32)
    local = jnp.where(first_chip, local, 0.0)
    part_own = (to_modes(nodes, basis_own) + local).astype(bf16)
    part_other = to_modes(nodes, basis_other).astype(bf16)
    low = jnp.where(first_core, part_own, part_other)
    high = jnp.where(first_core, part_other, part_own)
    sent = jnp.concatenate([low, high], axis=1)
    sent = sent.reshape(parts, row_count, col_count, col_width)
    sent = jnp.transpose(sent, (1, 2, 0, 3)).reshape(row_count * col_count, parts, col_width)
    every = lax.all_to_all(sent, ("row", "col"), 0, 0)
    every = every.reshape(row_count, col_count, parts, col_width)
    final = jnp.sum(every.astype(f32), axis=0).astype(bf16)
    return jnp.transpose(final, (1, 2, 0))


def solution(mesh):
    return jax.shard_map(
        on_device,
        mesh=mesh,
        in_specs=(P("row", None), P(None, "row"), P("row"), P(None, "col", "row"), P(), P()),
        out_specs=P(None, "col", "row"),
        check_vma=False,
    )
```

```python
import jax
import jax.numpy as jnp
from jax import lax
from jax.experimental import pallas as pl
from jax.experimental.pallas import tpu as pltpu
from jax.sharding import PartitionSpec as P

STEPS = 3
LOADS = 8

NN = (((1,), (0,)), ((), ()))
NT = (((1,), (1,)), ((), ()))


def product(left, right, dims):
    return lax.dot_general(left, right, dims, preferred_element_type=jnp.float32)


def first_kernel(field_ref, scale_ref, basis_ref, own_ref, other_ref, *held):
    *held, loaded = held
    core = lax.rem(lax.axis_index("row"), 2)
    width = held[0].shape[1]
    chunk = 2 * width // LOADS
    copies = []
    for h, which in enumerate((core, 1 - core)):
        for k in range(LOADS // 2):
            start = pl.multiple_of(which * width + k * chunk, chunk)
            copies.append(
                pltpu.make_async_copy(
                    basis_ref.at[:, pl.ds(start, chunk)],
                    held[h].at[:, pl.ds(k * chunk, chunk)],
                    loaded.at[h * (LOADS // 2) + k],
                )
            )
    for copy in copies:
        copy.start()
    nodes = jnp.zeros((field_ref.shape[1], held[0].shape[0]), jnp.float32)
    for k, copy in enumerate(copies):
        copy.wait()
        h, place = k // (LOADS // 2), pl.ds(k % (LOADS // 2) * chunk, chunk)
        nodes += product(field_ref[h, :, place], held[h][:, place], NT)
    half = nodes.shape[0] // 2
    scale = scale_ref[...]
    nodes = jnp.concatenate([scale * nodes[half:], -scale * nodes[:half]], axis=0)
    nodes = nodes.astype(jnp.bfloat16)
    for k in range(LOADS // 2):
        place = pl.ds(k * chunk, chunk)
        other_ref[:, place] = product(nodes, held[1][:, place], NN).astype(jnp.bfloat16)
        own_ref[:, place] = product(nodes, held[0][:, place], NN)


def first_operator(field, scale, basis):
    _, rows, width = field.shape
    nodes, modes = basis.shape
    in_vmem = pl.BlockSpec(memory_space=pltpu.VMEM)
    return pl.pallas_call(
        first_kernel,
        out_shape=(
            jax.ShapeDtypeStruct((rows, width), jnp.float32),
            jax.ShapeDtypeStruct((rows, width), jnp.bfloat16),
            jax.ShapeDtypeStruct((nodes, width), basis.dtype),
            jax.ShapeDtypeStruct((nodes, width), basis.dtype),
        ),
        in_specs=[in_vmem, in_vmem, pl.BlockSpec(memory_space=pl.ANY)],
        out_specs=(in_vmem,) * 4,
        scratch_shapes=[pltpu.SemaphoreType.DMA((LOADS,))],
        compiler_params=pltpu.CompilerParams(vmem_limit_bytes=44 << 20),
        cost_estimate=pl.CostEstimate(
            flops=4 * rows * modes * nodes, bytes_accessed=2 * modes * nodes, transcendentals=0
        ),
    )(field, scale, basis)


def turn_kernel(basis_ref, turned_ref):
    turned_ref[...] = basis_ref[...].T


def turned(basis, block=512):
    nodes, width = basis.shape
    return pl.pallas_call(
        turn_kernel,
        out_shape=jax.ShapeDtypeStruct((width, nodes), basis.dtype),
        grid=(width // block,),
        in_specs=[pl.BlockSpec((nodes, block), lambda j: (0, j))],
        out_specs=pl.BlockSpec((block, nodes), lambda j: (j, 0)),
        compiler_params=pltpu.CompilerParams(vmem_limit_bytes=10 << 20),
        cost_estimate=pl.CostEstimate(
            flops=0, bytes_accessed=4 * width * nodes, transcendentals=0
        ),
    )(basis)


def on_device(mode_basis, node_coords, quad_weights, magnetization, decay_rates, directions):
    row_count = lax.axis_size("row")
    col_count = lax.axis_size("col")
    row_index = lax.axis_index("row")
    col_index = lax.axis_index("col")
    core = row_index % 2
    mode_count = mode_basis.shape[1]
    node_local = mode_basis.shape[0]
    parts, col_width, own_waves = magnetization.shape
    columns = 2 * row_count
    width = mode_count // 2
    f32, bf16 = jnp.float32, jnp.bfloat16

    def move(array, target):
        return lax.ppermute(array, "row", [(r, target(r)) for r in range(row_count)])

    def to_other_core(array):
        return move(array, lambda r: r ^ 1)

    def along_y(array):
        return move(array, lambda r: r ^ 8)

    def along_z(array, hops):
        return move(array, lambda r: (r & 9) | ((r + 2 * hops) & 6))

    def over_chips(total):
        total = total + along_y(total.astype(bf16)).astype(f32)
        sent = total.astype(bf16)
        for hops in (1, 3, 2):
            total = total + along_z(sent, hops).astype(f32)
        return total

    mine = lax.dynamic_index_in_dim(
        directions.reshape(2 * STEPS, 3, row_count, own_waves), col_index, 3, keepdims=False
    )
    moments = node_coords * quad_weights[None, :]
    weights = jnp.sum(mine[:, :, :, None] * moments[None, :, None, :], axis=1)

    sent = jnp.transpose(magnetization, (2, 0, 1))
    sent = jnp.broadcast_to(sent[None], (row_count,) + sent.shape)
    sent = sent.reshape(row_count * col_count, parts, col_width)
    first_core, first_chip = core == 0, row_index < 2

    def half_of(array, which, axis):
        return lax.dynamic_slice_in_dim(array, which * width, width, axis)

    rates = jnp.stack([half_of(decay_rates, core, 0), half_of(decay_rates, 1 - core, 0)])
    sent, rates, first_core, first_chip = lax.optimization_barrier(
        (sent, rates, first_core, first_chip)
    )
    rates = rates[:1]
    every = lax.all_to_all(sent, ("row", "col"), 0, 0)
    every = every.reshape(row_count, col_count, parts, col_width)
    every = lax.optimization_barrier(
        jnp.transpose(every, (2, 0, 1, 3)).reshape(columns, mode_count)
    )

    def mixed(nodes, half_step):
        factor = 0.5 if half_step % 2 == 0 else 1.0
        scale = factor * weights[half_step]
        real, imag = nodes[:row_count], nodes[row_count:]
        rows = jnp.concatenate([scale * imag, -scale * real], axis=0)
        return lax.optimization_barrier(rows.astype(bf16))

    field = half_of(every, core, 1)
    both = jnp.stack([field, half_of(every, 1 - core, 1)])

    kept, sent, basis_own, basis_other = first_operator(both, 0.5 * weights[0], mode_basis)
    turned_own, turned_other = turned(basis_own), turned(basis_other)
    sums = over_chips(kept + to_other_core(sent).astype(f32))

    def weighted(own, other, half_step):
        kept = lax.optimization_barrier(product(own, turned_own, NN))
        return mixed(kept + product(other, turned_other, NN), half_step)

    def summed(nodes):
        arrived = to_other_core(product(nodes, basis_other, NN).astype(bf16))
        kept = lax.optimization_barrier(product(nodes, basis_own, NN))
        return over_chips(kept + arrived.astype(f32))

    for step in range(STEPS):
        if step > 0:
            sums = summed(weighted(field, to_other_core(field), 2 * step))
        half = (sums + (1.0 - 0.5 * rates) * field.astype(f32)).astype(bf16)
        nodes = weighted(half, to_other_core(half), 2 * step + 1)
        if step + 1 < STEPS:
            update = summed(nodes) + (0.0 - 1.0 * rates) * half.astype(f32)
            field = (field.astype(f32) + update).astype(bf16)

    local = field.astype(f32) + (0.0 - 1.0 * rates) * half.astype(f32)
    local = jnp.where(first_chip, local, 0.0)
    part_own = (product(nodes, basis_own, NN) + local).astype(bf16)
    part_other = product(nodes, basis_other, NN).astype(bf16)
    low = jnp.where(first_core, part_own, part_other)
    high = jnp.where(first_core, part_other, part_own)
    sent = jnp.concatenate([low, high], axis=1)
    sent = sent.reshape(parts, row_count, col_count, col_width)
    sent = jnp.transpose(sent, (1, 2, 0, 3)).reshape(row_count * col_count, parts, col_width)
    every = lax.all_to_all(sent, ("row", "col"), 0, 0)
    every = every.reshape(row_count, col_count, parts, col_width)
    final = jnp.sum(every.astype(f32), axis=0).astype(bf16)
    return jnp.transpose(final, (1, 2, 0))


def solution(mesh):
    return jax.shard_map(
        on_device,
        mesh=mesh,
        in_specs=(P("row", None), P(None, "row"), P("row"), P(None, "col", "row"), P(), P()),
        out_specs=P(None, "col", "row"),
        check_vma=False,
    )
```

```python
import jax
import jax.numpy as jnp
from jax import lax
from jax.experimental import pallas as pl
from jax.experimental.pallas import tpu as pltpu
from jax.sharding import PartitionSpec as P

STEPS = 3
LOADS = 8

NN = (((1,), (0,)), ((), ()))
NT = (((1,), (1,)), ((), ()))


def product(left, right, dims):
    return lax.dot_general(left, right, dims, preferred_element_type=jnp.float32)


def first_kernel(field_ref, scale_ref, basis_ref, own_ref, other_ref, *held):
    *held, loaded = held
    core = lax.rem(lax.axis_index("row"), 2)
    width = held[0].shape[1]
    chunk = 2 * width // LOADS
    copies = []
    for h, which in enumerate((core, 1 - core)):
        for k in range(LOADS // 2):
            start = pl.multiple_of(which * width + k * chunk, chunk)
            copies.append(
                pltpu.make_async_copy(
                    basis_ref.at[:, pl.ds(start, chunk)],
                    held[h].at[:, pl.ds(k * chunk, chunk)],
                    loaded.at[h * (LOADS // 2) + k],
                )
            )
    for copy in copies:
        copy.start()
    nodes = jnp.zeros((field_ref.shape[1], held[0].shape[0]), jnp.float32)
    for k, copy in enumerate(copies):
        copy.wait()
        h, place = k // (LOADS // 2), pl.ds(k % (LOADS // 2) * chunk, chunk)
        nodes += product(field_ref[h, :, place], held[h][:, place], NT)
    half = nodes.shape[0] // 2
    scale = scale_ref[...]
    nodes = jnp.concatenate([scale * nodes[half:], -scale * nodes[:half]], axis=0)
    nodes = nodes.astype(jnp.bfloat16)
    for k in range(LOADS // 2):
        place = pl.ds(k * chunk, chunk)
        other_ref[:, place] = product(nodes, held[1][:, place], NN).astype(jnp.bfloat16)
        own_ref[:, place] = product(nodes, held[0][:, place], NN)


def first_operator(field, scale, basis):
    _, rows, width = field.shape
    nodes, modes = basis.shape
    in_vmem = pl.BlockSpec(memory_space=pltpu.VMEM)
    return pl.pallas_call(
        first_kernel,
        out_shape=(
            jax.ShapeDtypeStruct((rows, width), jnp.float32),
            jax.ShapeDtypeStruct((rows, width), jnp.bfloat16),
            jax.ShapeDtypeStruct((nodes, width), basis.dtype),
            jax.ShapeDtypeStruct((nodes, width), basis.dtype),
        ),
        in_specs=[in_vmem, in_vmem, pl.BlockSpec(memory_space=pl.ANY)],
        out_specs=(in_vmem,) * 4,
        scratch_shapes=[pltpu.SemaphoreType.DMA((LOADS,))],
        compiler_params=pltpu.CompilerParams(vmem_limit_bytes=44 << 20),
        cost_estimate=pl.CostEstimate(
            flops=4 * rows * modes * nodes, bytes_accessed=2 * modes * nodes, transcendentals=0
        ),
    )(field, scale, basis)


def turn_kernel(basis_ref, turned_ref):
    turned_ref[...] = basis_ref[...].T


def turned(basis, block=512):
    nodes, width = basis.shape
    return pl.pallas_call(
        turn_kernel,
        out_shape=jax.ShapeDtypeStruct((width, nodes), basis.dtype),
        grid=(width // block,),
        in_specs=[pl.BlockSpec((nodes, block), lambda j: (0, j))],
        out_specs=pl.BlockSpec((block, nodes), lambda j: (j, 0)),
        compiler_params=pltpu.CompilerParams(vmem_limit_bytes=10 << 20),
        cost_estimate=pl.CostEstimate(
            flops=0, bytes_accessed=4 * width * nodes, transcendentals=0
        ),
    )(basis)


def spread_kernel(waves_ref, sent_ref):
    for wave in range(waves_ref.shape[1]):
        for part in range(waves_ref.shape[0]):
            line = waves_ref[part, wave : wave + 1, :]
            sent_ref[:, wave, part : part + 1, :] = jnp.broadcast_to(
                line[None], (sent_ref.shape[0],) + line.shape
            )


def spread(waves, row_count):
    parts, waves_here, width = waves.shape
    return pl.pallas_call(
        spread_kernel,
        out_shape=jax.ShapeDtypeStruct((row_count, waves_here, parts, width), waves.dtype),
        compiler_params=pltpu.CompilerParams(vmem_limit_bytes=8 << 20),
    )(waves)


def gather_kernel(arrived_ref, final_ref):
    total = jnp.sum(arrived_ref[...].astype(jnp.float32), axis=0)
    for part in range(final_ref.shape[0]):
        final_ref[part] = total[:, part, :].astype(final_ref.dtype)


def gathered(arrived):
    _, waves_here, parts, width = arrived.shape
    return pl.pallas_call(
        gather_kernel,
        out_shape=jax.ShapeDtypeStruct((parts, waves_here, width), arrived.dtype),
        compiler_params=pltpu.CompilerParams(vmem_limit_bytes=8 << 20),
    )(arrived)


def on_device(mode_basis, node_coords, quad_weights, magnetization, decay_rates, directions):
    row_count = lax.axis_size("row")
    col_count = lax.axis_size("col")
    row_index = lax.axis_index("row")
    col_index = lax.axis_index("col")
    core = row_index % 2
    mode_count = mode_basis.shape[1]
    node_local = mode_basis.shape[0]
    parts, col_width, own_waves = magnetization.shape
    columns = 2 * row_count
    width = mode_count // 2
    f32, bf16 = jnp.float32, jnp.bfloat16

    def move(array, target):
        return lax.ppermute(array, "row", [(r, target(r)) for r in range(row_count)])

    def to_other_core(array):
        return move(array, lambda r: r ^ 1)

    def along_y(array):
        return move(array, lambda r: r ^ 8)

    def along_z(array, hops):
        return move(array, lambda r: (r & 9) | ((r + 2 * hops) & 6))

    def over_chips(total):
        total = total + along_y(total.astype(bf16)).astype(f32)
        sent = total.astype(bf16)
        for hops in (1, 3, 2):
            total = total + along_z(sent, hops).astype(f32)
        return total

    mine = lax.dynamic_index_in_dim(
        directions.reshape(2 * STEPS, 3, row_count, own_waves), col_index, 3, keepdims=False
    )
    moments = node_coords * quad_weights[None, :]
    weights = jnp.sum(mine[:, :, :, None] * moments[None, :, None, :], axis=1)

    sent = spread(jnp.transpose(magnetization, (0, 2, 1)), row_count)
    sent = sent.reshape(row_count * col_count, parts, col_width)
    first_core, first_chip = core == 0, row_index < 2

    def half_of(array, which, axis):
        return lax.dynamic_slice_in_dim(array, which * width, width, axis)

    rates = half_of(decay_rates, core, 0)[None, :]
    sent, first_core, first_chip = lax.optimization_barrier((sent, first_core, first_chip))
    every = lax.all_to_all(sent, ("row", "col"), 0, 0)
    every = every.reshape(row_count, col_count, parts, col_width)
    every = lax.optimization_barrier(
        jnp.transpose(every, (2, 0, 1, 3)).reshape(columns, mode_count)
    )

    def mixed(nodes, half_step):
        factor = 0.5 if half_step % 2 == 0 else 1.0
        scale = factor * weights[half_step]
        real, imag = nodes[:row_count], nodes[row_count:]
        rows = jnp.concatenate([scale * imag, -scale * real], axis=0)
        return lax.optimization_barrier(rows.astype(bf16))

    field = half_of(every, core, 1)
    both = jnp.stack([field, half_of(every, 1 - core, 1)])

    kept, sent, basis_own, basis_other = first_operator(both, 0.5 * weights[0], mode_basis)
    turned_own, turned_other = turned(basis_own), turned(basis_other)
    sums = over_chips(kept + to_other_core(sent).astype(f32))

    def weighted(own, other, half_step):
        kept = lax.optimization_barrier(product(own, turned_own, NN))
        return mixed(kept + product(other, turned_other, NN), half_step)

    def summed(nodes):
        arrived = to_other_core(product(nodes, basis_other, NN).astype(bf16))
        kept = lax.optimization_barrier(product(nodes, basis_own, NN))
        return over_chips(kept + arrived.astype(f32))

    for step in range(STEPS):
        if step > 0:
            sums = summed(weighted(field, to_other_core(field), 2 * step))
        half = (sums + (1.0 - 0.5 * rates) * field.astype(f32)).astype(bf16)
        nodes = weighted(half, to_other_core(half), 2 * step + 1)
        if step + 1 < STEPS:
            update = summed(nodes) + (0.0 - 1.0 * rates) * half.astype(f32)
            field = (field.astype(f32) + update).astype(bf16)

    local = field.astype(f32) + (0.0 - 1.0 * rates) * half.astype(f32)
    local = jnp.where(first_chip, local, 0.0)
    part_own = (product(nodes, basis_own, NN) + local).astype(bf16)
    part_other = product(nodes, basis_other, NN).astype(bf16)
    low = jnp.where(first_core, part_own, part_other)
    high = jnp.where(first_core, part_other, part_own)
    sent = jnp.concatenate([low, high], axis=1)
    sent = sent.reshape(parts, row_count, col_count, col_width)
    sent = jnp.transpose(sent, (1, 2, 0, 3)).reshape(row_count * col_count, parts, col_width)
    every = lax.all_to_all(sent, ("row", "col"), 0, 0)
    every = every.reshape(row_count, col_count, parts, col_width)
    return jnp.transpose(gathered(every), (0, 2, 1))


def solution(mesh):
    return jax.shard_map(
        on_device,
        mesh=mesh,
        in_specs=(P("row", None), P(None, "row"), P("row"), P(None, "col", "row"), P(), P()),
        out_specs=P(None, "col", "row"),
        check_vma=False,
    )
```

```python
import jax
import jax.numpy as jnp
from jax import lax
from jax.experimental import pallas as pl
from jax.experimental.pallas import tpu as pltpu
from jax.sharding import PartitionSpec as P

STEPS = 3

NN = (((1,), (0,)), ((), ()))
NT = (((1,), (1,)), ((), ()))


def product(left, right, dims):
    return lax.dot_general(left, right, dims, preferred_element_type=jnp.float32)


def turn_kernel(from_ref, basis_ref, turned_ref):
    turned_ref[...] = basis_ref[...].T


def turned(basis, start, block=512):
    nodes, modes = basis.shape
    width = modes // 2
    return pl.pallas_call(
        turn_kernel,
        out_shape=jax.ShapeDtypeStruct((width, nodes), basis.dtype),
        grid_spec=pltpu.PrefetchScalarGridSpec(
            num_scalar_prefetch=1,
            grid=(width // block,),
            in_specs=[pl.BlockSpec((nodes, block), lambda j, w: (0, w[0] // block + j))],
            out_specs=pl.BlockSpec((block, nodes), lambda j, w: (j, 0)),
        ),
        compiler_params=pltpu.CompilerParams(vmem_limit_bytes=10 << 20),
        cost_estimate=pl.CostEstimate(
            flops=0, bytes_accessed=4 * width * nodes, transcendentals=0
        ),
    )(start, basis)


def spread_kernel(waves_ref, sent_ref):
    for wave in range(waves_ref.shape[1]):
        for part in range(waves_ref.shape[0]):
            line = waves_ref[part, wave : wave + 1, :]
            sent_ref[:, wave, part : part + 1, :] = jnp.broadcast_to(
                line[None], (sent_ref.shape[0],) + line.shape
            )


def spread(waves, row_count):
    parts, waves_here, width = waves.shape
    return pl.pallas_call(
        spread_kernel,
        out_shape=jax.ShapeDtypeStruct((row_count, waves_here, parts, width), waves.dtype),
        compiler_params=pltpu.CompilerParams(vmem_limit_bytes=32 << 20),
        cost_estimate=pl.CostEstimate(flops=1 << 34, bytes_accessed=1 << 20, transcendentals=0),
    )(waves)


def weights_kernel(coords_ref, quad_ref, turns_ref, weights_ref):
    half_steps, axes, waves = turns_ref.shape
    rows = weights_ref.shape[1]
    shape = (rows, waves)
    lane = lax.broadcasted_iota(jnp.int32, shape, 1)
    wanted = lax.broadcasted_iota(jnp.int32, shape, 0) * (waves // rows)
    wanted += lax.axis_index("col")
    moments = coords_ref[...] * quad_ref[...]
    for a in range(half_steps):
        total = None
        for k in range(axes):
            line = jnp.broadcast_to(turns_ref[a, k : k + 1, :], shape)
            turn = jnp.sum(jnp.where(lane == wanted, line, 0.0), axis=1, keepdims=True)
            term = turn * moments[k : k + 1, :]
            total = term if total is None else total + term
        weights_ref[a] = total


def node_weights(coords, quad, turns, row_count):
    return pl.pallas_call(
        weights_kernel,
        out_shape=jax.ShapeDtypeStruct((turns.shape[0], row_count, coords.shape[1]), coords.dtype),
        compiler_params=pltpu.CompilerParams(vmem_limit_bytes=16 << 20),
    )(coords, quad, turns)


def gather_kernel(arrived_ref, final_ref):
    total = jnp.sum(arrived_ref[...].astype(jnp.float32), axis=0)
    for part in range(final_ref.shape[0]):
        final_ref[part] = total[:, part, :].astype(final_ref.dtype)


def gathered(arrived):
    _, waves_here, parts, width = arrived.shape
    return pl.pallas_call(
        gather_kernel,
        out_shape=jax.ShapeDtypeStruct((parts, waves_here, width), arrived.dtype),
        compiler_params=pltpu.CompilerParams(vmem_limit_bytes=8 << 20),
    )(arrived)


def on_device(mode_basis, node_coords, quad_weights, magnetization, decay_rates, directions):
    row_count = lax.axis_size("row")
    col_count = lax.axis_size("col")
    row_index = lax.axis_index("row")
    col_index = lax.axis_index("col")
    core = row_index % 2
    mode_count = mode_basis.shape[1]
    node_local = mode_basis.shape[0]
    parts, col_width, own_waves = magnetization.shape
    columns = 2 * row_count
    width = mode_count // 2
    f32, bf16 = jnp.float32, jnp.bfloat16

    def move(array, target):
        return lax.ppermute(array, "row", [(r, target(r)) for r in range(row_count)])

    def to_other_core(array):
        return move(array, lambda r: r ^ 1)

    def along_y(array):
        return move(array, lambda r: r ^ 8)

    def along_z(array, hops):
        return move(array, lambda r: (r & 9) | ((r + 2 * hops) & 6))

    def over_chips(total):
        total = total + along_y(total.astype(bf16)).astype(f32)
        sent = total.astype(bf16)
        for hops in (1, 3, 2):
            total = total + along_z(sent, hops).astype(f32)
        return total

    waves = jnp.transpose(magnetization, (0, 2, 1))
    own_from, other_from = (core * width).reshape(1), ((1 - core) * width).reshape(1)
    first_core, first_chip = core == 0, row_index < 2
    waves, own_from, other_from, first_core, first_chip = lax.optimization_barrier(
        (waves, own_from, other_from, first_core, first_chip)
    )
    sent = spread(waves, row_count)
    sent = sent.reshape(row_count * col_count, parts, col_width)
    def half_of(array, which, axis):
        starts = [jnp.int32(0)] * array.ndim
        sizes = list(array.shape)
        starts[axis], sizes[axis] = which * width, width
        return lax.dynamic_slice_p.bind(array, *starts, slice_sizes=tuple(sizes))

    rates = half_of(decay_rates, core, 0)[None, :]
    every = lax.all_to_all(sent, ("row", "col"), 0, 0)
    every = every.reshape(row_count, col_count, parts, col_width)
    every = jnp.transpose(every, (2, 0, 1, 3)).reshape(columns, mode_count)
    every, coords, quad, turns = lax.optimization_barrier(
        (every, node_coords, quad_weights[None, :], directions)
    )
    weights = node_weights(coords, quad, turns, row_count)

    def mixed(nodes, half_step):
        factor = 0.5 if half_step % 2 == 0 else 1.0
        scale = factor * weights[half_step]
        real, imag = nodes[:row_count], nodes[row_count:]
        rows = jnp.concatenate([scale * imag, -scale * real], axis=0)
        return lax.optimization_barrier(rows.astype(bf16))

    field = half_of(every, core, 1)
    basis_own, basis_other = half_of(mode_basis, core, 1), half_of(mode_basis, 1 - core, 1)

    kept = lax.optimization_barrier(product(field, basis_own, NT))
    nodes = mixed(kept + product(half_of(every, 1 - core, 1), basis_other, NT), 0)
    sent = product(nodes, basis_other, NN).astype(bf16)
    kept = lax.optimization_barrier(product(nodes, basis_own, NN))
    turned_own, turned_other = turned(mode_basis, own_from), turned(mode_basis, other_from)
    sums = over_chips(kept + to_other_core(sent).astype(f32))

    def weighted(own, other, half_step):
        kept = lax.optimization_barrier(product(own, turned_own, NN))
        return mixed(kept + product(other, turned_other, NN), half_step)

    def summed(nodes):
        arrived = to_other_core(product(nodes, basis_other, NN).astype(bf16))
        kept = lax.optimization_barrier(product(nodes, basis_own, NN))
        return over_chips(kept + arrived.astype(f32))

    for step in range(STEPS):
        if step > 0:
            sums = summed(weighted(field, to_other_core(field), 2 * step))
        half = (sums + (1.0 - 0.5 * rates) * field.astype(f32)).astype(bf16)
        nodes = weighted(half, to_other_core(half), 2 * step + 1)
        if step + 1 < STEPS:
            update = summed(nodes) + (0.0 - 1.0 * rates) * half.astype(f32)
            field = (field.astype(f32) + update).astype(bf16)

    local = field.astype(f32) + (0.0 - 1.0 * rates) * half.astype(f32)
    local = jnp.where(first_chip, local, 0.0)
    part_own = (product(nodes, basis_own, NN) + local).astype(bf16)
    part_other = product(nodes, basis_other, NN).astype(bf16)
    low = jnp.where(first_core, part_own, part_other)
    high = jnp.where(first_core, part_other, part_own)
    sent = jnp.concatenate([low, high], axis=1)
    sent = sent.reshape(parts, row_count, col_count, col_width)
    sent = jnp.transpose(sent, (1, 2, 0, 3)).reshape(row_count * col_count, parts, col_width)
    every = lax.all_to_all(sent, ("row", "col"), 0, 0)
    every = every.reshape(row_count, col_count, parts, col_width)
    return jnp.transpose(gathered(every), (0, 2, 1))


def solution(mesh):
    return jax.shard_map(
        on_device,
        mesh=mesh,
        in_specs=(P("row", None), P(None, "row"), P("row"), P(None, "col", "row"), P(), P()),
        out_specs=P(None, "col", "row"),
        check_vma=False,
    )
```

```python
import jax
import jax.numpy as jnp
from jax import lax
from jax.experimental import pallas as pl
from jax.experimental.pallas import tpu as pltpu
from jax.sharding import PartitionSpec as P

STEPS = 3

NN = (((1,), (0,)), ((), ()))
NT = (((1,), (1,)), ((), ()))


def product(left, right, dims):
    return lax.dot_general(left, right, dims, preferred_element_type=jnp.float32)


def turn_kernel(from_ref, basis_ref, turned_ref):
    turned_ref[...] = basis_ref[...].T


def turned(basis, start, block=512):
    nodes, modes = basis.shape
    width = modes // 2
    return pl.pallas_call(
        turn_kernel,
        out_shape=jax.ShapeDtypeStruct((width, nodes), basis.dtype),
        grid_spec=pltpu.PrefetchScalarGridSpec(
            num_scalar_prefetch=1,
            grid=(width // block,),
            in_specs=[pl.BlockSpec((nodes, block), lambda j, w: (0, w[0] // block + j))],
            out_specs=pl.BlockSpec((block, nodes), lambda j, w: (j, 0)),
        ),
        compiler_params=pltpu.CompilerParams(vmem_limit_bytes=10 << 20),
        cost_estimate=pl.CostEstimate(
            flops=0, bytes_accessed=4 * width * nodes, transcendentals=0
        ),
    )(start, basis)


def spread_kernel(waves_ref, sent_ref):
    for wave in range(waves_ref.shape[1]):
        for part in range(waves_ref.shape[0]):
            line = waves_ref[part, wave : wave + 1, :]
            sent_ref[:, wave, part : part + 1, :] = jnp.broadcast_to(
                line[None], (sent_ref.shape[0],) + line.shape
            )


def spread(waves, row_count):
    parts, waves_here, width = waves.shape
    return pl.pallas_call(
        spread_kernel,
        out_shape=jax.ShapeDtypeStruct((row_count, waves_here, parts, width), waves.dtype),
        compiler_params=pltpu.CompilerParams(vmem_limit_bytes=32 << 20),
        cost_estimate=pl.CostEstimate(flops=1 << 34, bytes_accessed=1 << 20, transcendentals=0),
    )(waves)


def weights_kernel(coords_ref, quad_ref, turns_ref, weights_ref):
    half_steps, axes, waves = turns_ref.shape
    rows = weights_ref.shape[1]
    shape = (rows, waves)
    lane = lax.broadcasted_iota(jnp.int32, shape, 1)
    wanted = lax.broadcasted_iota(jnp.int32, shape, 0) * (waves // rows)
    wanted += lax.axis_index("col")
    moments = coords_ref[...] * quad_ref[...]
    for a in range(half_steps):
        total = None
        for k in range(axes):
            line = jnp.broadcast_to(turns_ref[a, k : k + 1, :], shape)
            turn = jnp.sum(jnp.where(lane == wanted, line, 0.0), axis=1, keepdims=True)
            term = turn * moments[k : k + 1, :]
            total = term if total is None else total + term
        weights_ref[a] = total


def node_weights(coords, quad, turns, row_count):
    return pl.pallas_call(
        weights_kernel,
        out_shape=jax.ShapeDtypeStruct((turns.shape[0], row_count, coords.shape[1]), coords.dtype),
        compiler_params=pltpu.CompilerParams(vmem_limit_bytes=16 << 20),
    )(coords, quad, turns)


def gather_kernel(arrived_ref, final_ref):
    total = jnp.sum(arrived_ref[...].astype(jnp.float32), axis=0)
    for part in range(final_ref.shape[0]):
        final_ref[part] = total[:, part, :].astype(final_ref.dtype)


def gathered(arrived):
    _, waves_here, parts, width = arrived.shape
    return pl.pallas_call(
        gather_kernel,
        out_shape=jax.ShapeDtypeStruct((parts, waves_here, width), arrived.dtype),
        compiler_params=pltpu.CompilerParams(vmem_limit_bytes=8 << 20),
    )(arrived)


def on_device(mode_basis, node_coords, quad_weights, magnetization, decay_rates, directions):
    row_count = lax.axis_size("row")
    col_count = lax.axis_size("col")
    row_index = lax.axis_index("row")
    col_index = lax.axis_index("col")
    core = row_index % 2
    mode_count = mode_basis.shape[1]
    node_local = mode_basis.shape[0]
    parts, col_width, own_waves = magnetization.shape
    columns = 2 * row_count
    width = mode_count // 2
    f32, bf16 = jnp.float32, jnp.bfloat16

    def move(array, target):
        return lax.ppermute(array, "row", [(r, target(r)) for r in range(row_count)])

    def to_other_core(array):
        return move(array, lambda r: r ^ 1)

    def along_y(array):
        return move(array, lambda r: r ^ 8)

    def along_z(array, hops):
        return move(array, lambda r: r ^ (2 * hops))

    def over_chips(total, beside=None):
        arrived = along_y(total.astype(bf16))
        if beside is not None:
            arrived, _ = lax.optimization_barrier((arrived, beside))
        total = total + arrived.astype(f32)
        sent = total.astype(bf16)
        for hops in (1, 3, 2):
            total = total + along_z(sent, hops).astype(f32)
        return total

    waves = jnp.transpose(magnetization, (0, 2, 1))
    own_from, other_from = (core * width).reshape(1), ((1 - core) * width).reshape(1)
    first_core, first_chip = core == 0, row_index < 2
    waves, own_from, other_from, first_core, first_chip = lax.optimization_barrier(
        (waves, own_from, other_from, first_core, first_chip)
    )
    sent = spread(waves, row_count)
    sent = sent.reshape(row_count * col_count, parts, col_width)
    def half_of(array, which, axis):
        starts = [jnp.int32(0)] * array.ndim
        sizes = list(array.shape)
        starts[axis], sizes[axis] = which * width, width
        return lax.dynamic_slice_p.bind(array, *starts, slice_sizes=tuple(sizes))

    rates = half_of(decay_rates, core, 0)[None, :]
    every = lax.all_to_all(sent, ("row", "col"), 0, 0)
    every = every.reshape(row_count, col_count, parts, col_width)
    every = jnp.transpose(every, (2, 0, 1, 3)).reshape(columns, mode_count)
    every, coords, quad, turns = lax.optimization_barrier(
        (every, node_coords, quad_weights[None, :], directions)
    )
    weights = node_weights(coords, quad, turns, row_count)

    def mixed(nodes, half_step):
        factor = 0.5 if half_step % 2 == 0 else 1.0
        scale = factor * weights[half_step]
        real, imag = nodes[:row_count], nodes[row_count:]
        rows = jnp.concatenate([scale * imag, -scale * real], axis=0)
        return lax.optimization_barrier(rows.astype(bf16))

    field = half_of(every, core, 1)
    basis_own, basis_other = half_of(mode_basis, core, 1), half_of(mode_basis, 1 - core, 1)

    kept = lax.optimization_barrier(product(field, basis_own, NT))
    nodes = mixed(kept + product(half_of(every, 1 - core, 1), basis_other, NT), 0)
    sent = product(nodes, basis_other, NN).astype(bf16)
    kept = lax.optimization_barrier(product(nodes, basis_own, NN))
    turned_own, turned_other = turned(mode_basis, own_from), turned(mode_basis, other_from)
    sums = over_chips(kept + to_other_core(sent).astype(f32), turned_own)

    def weighted(own, other, half_step):
        kept = lax.optimization_barrier(product(own, turned_own, NN))
        return mixed(kept + product(other, turned_other, NN), half_step)

    def summed(nodes):
        arrived = to_other_core(product(nodes, basis_other, NN).astype(bf16))
        kept = lax.optimization_barrier(product(nodes, basis_own, NN))
        return over_chips(kept + arrived.astype(f32))

    for step in range(STEPS):
        if step > 0:
            sums = summed(weighted(field, to_other_core(field), 2 * step))
        half = (sums + (1.0 - 0.5 * rates) * field.astype(f32)).astype(bf16)
        nodes = weighted(half, to_other_core(half), 2 * step + 1)
        if step + 1 < STEPS:
            update = summed(nodes) + (0.0 - 1.0 * rates) * half.astype(f32)
            field = (field.astype(f32) + update).astype(bf16)

    local = field.astype(f32) + (0.0 - 1.0 * rates) * half.astype(f32)
    local = jnp.where(first_chip, local, 0.0)
    part_own = (product(nodes, basis_own, NN) + local).astype(bf16)
    part_other = product(nodes, basis_other, NN).astype(bf16)
    low = jnp.where(first_core, part_own, part_other)
    high = jnp.where(first_core, part_other, part_own)
    sent = jnp.concatenate([low, high], axis=1)
    sent = sent.reshape(parts, row_count, col_count, col_width)
    sent = jnp.transpose(sent, (1, 2, 0, 3)).reshape(row_count * col_count, parts, col_width)
    every = lax.all_to_all(sent, ("row", "col"), 0, 0)
    every = every.reshape(row_count, col_count, parts, col_width)
    return jnp.transpose(gathered(every), (0, 2, 1))


def solution(mesh):
    return jax.shard_map(
        on_device,
        mesh=mesh,
        in_specs=(P("row", None), P(None, "row"), P("row"), P(None, "col", "row"), P(), P()),
        out_specs=P(None, "col", "row"),
        check_vma=False,
    )
```

```python
import jax
import jax.numpy as jnp
from jax import lax
from jax.experimental import pallas as pl
from jax.experimental.pallas import tpu as pltpu
from jax.sharding import PartitionSpec as P

STEPS = 3

NN = (((1,), (0,)), ((), ()))
NT = (((1,), (1,)), ((), ()))


def product(left, right, dims):
    return lax.dot_general(left, right, dims, preferred_element_type=jnp.float32)


def turn_kernel(from_ref, basis_ref, turned_ref):
    turned_ref[...] = basis_ref[...].T


def turned(basis, start, block=512):
    nodes, modes = basis.shape
    width = modes // 2
    return pl.pallas_call(
        turn_kernel,
        out_shape=jax.ShapeDtypeStruct((width, nodes), basis.dtype),
        grid_spec=pltpu.PrefetchScalarGridSpec(
            num_scalar_prefetch=1,
            grid=(width // block,),
            in_specs=[pl.BlockSpec((nodes, block), lambda j, w: (0, w[0] // block + j))],
            out_specs=pl.BlockSpec((block, nodes), lambda j, w: (j, 0)),
        ),
        compiler_params=pltpu.CompilerParams(vmem_limit_bytes=10 << 20),
        cost_estimate=pl.CostEstimate(
            flops=0, bytes_accessed=4 * width * nodes, transcendentals=0
        ),
    )(start, basis)


def flip_kernel(array_ref, turned_ref):
    turned_ref[...] = array_ref[...].T


def flipped(array, block=512):
    rows, width = array.shape
    return pl.pallas_call(
        flip_kernel,
        out_shape=jax.ShapeDtypeStruct((width, rows), array.dtype),
        grid=(rows // block,),
        in_specs=[pl.BlockSpec((block, width), lambda j: (j, 0))],
        out_specs=pl.BlockSpec((width, block), lambda j: (0, j)),
        compiler_params=pltpu.CompilerParams(vmem_limit_bytes=10 << 20),
        cost_estimate=pl.CostEstimate(
            flops=0, bytes_accessed=4 * width * rows, transcendentals=0
        ),
    )(array)


def spread_kernel(waves_ref, sent_ref):
    for wave in range(waves_ref.shape[1]):
        for part in range(waves_ref.shape[0]):
            line = waves_ref[part, wave : wave + 1, :]
            sent_ref[:, wave, part : part + 1, :] = jnp.broadcast_to(
                line[None], (sent_ref.shape[0],) + line.shape
            )


def spread(waves, row_count):
    parts, waves_here, width = waves.shape
    return pl.pallas_call(
        spread_kernel,
        out_shape=jax.ShapeDtypeStruct((row_count, waves_here, parts, width), waves.dtype),
        compiler_params=pltpu.CompilerParams(vmem_limit_bytes=32 << 20),
        cost_estimate=pl.CostEstimate(flops=1 << 34, bytes_accessed=1 << 20, transcendentals=0),
    )(waves)


def weights_kernel(coords_ref, quad_ref, turns_ref, weights_ref):
    half_steps, axes, waves = turns_ref.shape
    rows = weights_ref.shape[1]
    shape = (rows, waves)
    lane = lax.broadcasted_iota(jnp.int32, shape, 1)
    wanted = lax.broadcasted_iota(jnp.int32, shape, 0) * (waves // rows)
    wanted += lax.axis_index("col")
    moments = coords_ref[...] * quad_ref[...]
    for a in range(half_steps):
        total = None
        for k in range(axes):
            line = jnp.broadcast_to(turns_ref[a, k : k + 1, :], shape)
            turn = jnp.sum(jnp.where(lane == wanted, line, 0.0), axis=1, keepdims=True)
            term = turn * moments[k : k + 1, :]
            total = term if total is None else total + term
        weights_ref[a] = total


def node_weights(coords, quad, turns, row_count):
    return pl.pallas_call(
        weights_kernel,
        out_shape=jax.ShapeDtypeStruct((turns.shape[0], row_count, coords.shape[1]), coords.dtype),
        compiler_params=pltpu.CompilerParams(vmem_limit_bytes=16 << 20),
    )(coords, quad, turns)


def gather_kernel(arrived_ref, final_ref):
    total = jnp.sum(arrived_ref[...].astype(jnp.float32), axis=0)
    for part in range(final_ref.shape[0]):
        final_ref[part] = total[:, part, :].astype(final_ref.dtype)


def gathered(arrived):
    _, waves_here, parts, width = arrived.shape
    return pl.pallas_call(
        gather_kernel,
        out_shape=jax.ShapeDtypeStruct((parts, waves_here, width), arrived.dtype),
        compiler_params=pltpu.CompilerParams(vmem_limit_bytes=8 << 20),
    )(arrived)


def on_device(mode_basis, node_coords, quad_weights, magnetization, decay_rates, directions):
    row_count = lax.axis_size("row")
    col_count = lax.axis_size("col")
    row_index = lax.axis_index("row")
    col_index = lax.axis_index("col")
    core = row_index % 2
    mode_count = mode_basis.shape[1]
    node_local = mode_basis.shape[0]
    parts, col_width, own_waves = magnetization.shape
    columns = 2 * row_count
    width = mode_count // 2
    f32, bf16 = jnp.float32, jnp.bfloat16

    def move(array, target):
        return lax.ppermute(array, "row", [(r, target(r)) for r in range(row_count)])

    def to_other_core(array):
        return move(array, lambda r: r ^ 1)

    def along_y(array):
        return move(array, lambda r: r ^ 8)

    def along_z(array, hops):
        return move(array, lambda r: r ^ (2 * hops))

    def over_chips(total, beside=None):
        arrived = along_y(total.astype(bf16))
        if beside is not None:
            arrived, _ = lax.optimization_barrier((arrived, beside))
        total = total + arrived.astype(f32)
        sent = total.astype(bf16)
        for hops in (1, 3, 2):
            total = total + along_z(sent, hops).astype(f32)
        return total

    waves = jnp.transpose(magnetization, (0, 2, 1))
    own_from, other_from = (core * width).reshape(1), ((1 - core) * width).reshape(1)
    first_core, first_chip = core == 0, row_index < 2
    waves, own_from, other_from, first_core, first_chip = lax.optimization_barrier(
        (waves, own_from, other_from, first_core, first_chip)
    )
    sent = spread(waves, row_count)
    sent = sent.reshape(row_count * col_count, parts, col_width)
    def half_of(array, which, axis):
        starts = [jnp.int32(0)] * array.ndim
        sizes = list(array.shape)
        starts[axis], sizes[axis] = which * width, width
        return lax.dynamic_slice_p.bind(array, *starts, slice_sizes=tuple(sizes))

    rates = half_of(decay_rates, core, 0)[None, :]
    every = lax.all_to_all(sent, ("row", "col"), 0, 0)
    every = every.reshape(row_count, col_count, parts, col_width)
    every = jnp.transpose(every, (2, 0, 1, 3)).reshape(columns, mode_count)
    every, coords, quad, turns = lax.optimization_barrier(
        (every, node_coords, quad_weights[None, :], directions)
    )
    weights = node_weights(coords, quad, turns, row_count)

    def mixed(nodes, half_step, weights=weights):
        factor = 0.5 if half_step % 2 == 0 else 1.0
        scale = factor * weights[half_step]
        real, imag = nodes[:row_count], nodes[row_count:]
        rows = jnp.concatenate([scale * imag, -scale * real], axis=0)
        return lax.optimization_barrier(rows.astype(bf16))

    field = half_of(every, core, 1)
    basis_own, basis_other = half_of(mode_basis, core, 1), half_of(mode_basis, 1 - core, 1)

    kept = lax.optimization_barrier(product(field, basis_own, NT))
    nodes = mixed(kept + product(half_of(every, 1 - core, 1), basis_other, NT), 0)
    sent = product(nodes, basis_other, NN).astype(bf16)
    kept = lax.optimization_barrier(product(nodes, basis_own, NN))
    turned_own, turned_other = turned(mode_basis, own_from), turned(mode_basis, other_from)
    sums = over_chips(kept + to_other_core(sent).astype(f32), turned_own)

    def weighted(own, other, half_step):
        kept = lax.optimization_barrier(product(own, turned_own, NN))
        return mixed(kept + product(other, turned_other, NN), half_step)

    def summed(nodes, beside):
        arrived = to_other_core(product(nodes, basis_other, NN).astype(bf16))
        kept = lax.optimization_barrier(product(nodes, basis_own, NN))
        return over_chips(kept + arrived.astype(f32), beside)

    turned_mate = to_other_core(turned_other)
    weights_mate = to_other_core(weights)
    basis_mate = flipped(turned_mate)

    def reduced(own, half_step):
        for_mate = lax.optimization_barrier(product(own, turned_mate, NN))
        arrived = to_other_core(for_mate.astype(bf16))
        for_own = lax.optimization_barrier(product(own, turned_own, NN))
        arrived_mate = to_other_core(for_own.astype(bf16))
        nodes = mixed(for_own + arrived.astype(f32), half_step)
        kept = lax.optimization_barrier(product(nodes, basis_own, NN))
        nodes = mixed(for_mate + arrived_mate.astype(f32), half_step, weights_mate)
        return kept + product(nodes, basis_mate, NN)

    for step in range(STEPS):
        if step > 0:
            sums = over_chips(reduced(field, 2 * step))
        half = (sums + (1.0 - 0.5 * rates) * field.astype(f32)).astype(bf16)
        if step == 0:
            sums = summed(weighted(half, to_other_core(half), 1), (basis_mate, weights_mate))
        elif step + 1 < STEPS:
            sums = over_chips(reduced(half, 2 * step + 1))
        if step + 1 < STEPS:
            update = sums + (0.0 - 1.0 * rates) * half.astype(f32)
            field = (field.astype(f32) + update).astype(bf16)

    local = field.astype(f32) + (0.0 - 1.0 * rates) * half.astype(f32)
    local = jnp.where(first_chip, local, 0.0)
    part_own = (reduced(half, 2 * STEPS - 1) + local).astype(bf16)
    part_other = jnp.zeros_like(part_own)
    low = jnp.where(first_core, part_own, part_other)
    high = jnp.where(first_core, part_other, part_own)
    sent = jnp.concatenate([low, high], axis=1)
    sent = sent.reshape(parts, row_count, col_count, col_width)
    sent = jnp.transpose(sent, (1, 2, 0, 3)).reshape(row_count * col_count, parts, col_width)
    every = lax.all_to_all(sent, ("row", "col"), 0, 0)
    every = every.reshape(row_count, col_count, parts, col_width)
    return jnp.transpose(gathered(every), (0, 2, 1))


def solution(mesh):
    return jax.shard_map(
        on_device,
        mesh=mesh,
        in_specs=(P("row", None), P(None, "row"), P("row"), P(None, "col", "row"), P(), P()),
        out_specs=P(None, "col", "row"),
        check_vma=False,
    )
```

```python
import jax
import jax.numpy as jnp
from jax import lax
from jax.experimental import pallas as pl
from jax.experimental.pallas import tpu as pltpu
from jax.sharding import PartitionSpec as P

STEPS = 3

NN = (((1,), (0,)), ((), ()))
NT = (((1,), (1,)), ((), ()))


def product(left, right, dims):
    return lax.dot_general(left, right, dims, preferred_element_type=jnp.float32)


def turn_kernel(from_ref, basis_ref, turned_ref):
    turned_ref[...] = basis_ref[...].T


def turned(basis, start, block=512):
    nodes, modes = basis.shape
    width = modes // 2
    return pl.pallas_call(
        turn_kernel,
        out_shape=jax.ShapeDtypeStruct((width, nodes), basis.dtype),
        grid_spec=pltpu.PrefetchScalarGridSpec(
            num_scalar_prefetch=1,
            grid=(width // block,),
            in_specs=[pl.BlockSpec((nodes, block), lambda j, w: (0, w[0] // block + j))],
            out_specs=pl.BlockSpec((block, nodes), lambda j, w: (j, 0)),
        ),
        compiler_params=pltpu.CompilerParams(vmem_limit_bytes=10 << 20),
        cost_estimate=pl.CostEstimate(
            flops=0, bytes_accessed=4 * width * nodes, transcendentals=0
        ),
    )(start, basis)


def spread_kernel(waves_ref, sent_ref):
    for wave in range(waves_ref.shape[1]):
        for part in range(waves_ref.shape[0]):
            line = waves_ref[part, wave : wave + 1, :]
            sent_ref[:, wave, part : part + 1, :] = jnp.broadcast_to(
                line[None], (sent_ref.shape[0],) + line.shape
            )


def spread(waves, row_count):
    parts, waves_here, width = waves.shape
    return pl.pallas_call(
        spread_kernel,
        out_shape=jax.ShapeDtypeStruct((row_count, waves_here, parts, width), waves.dtype),
        compiler_params=pltpu.CompilerParams(vmem_limit_bytes=32 << 20),
        cost_estimate=pl.CostEstimate(flops=1 << 34, bytes_accessed=1 << 20, transcendentals=0),
    )(waves)


def weights_kernel(coords_ref, quad_ref, turns_ref, weights_ref):
    half_steps, axes, waves = turns_ref.shape
    rows = weights_ref.shape[1] // 2
    shape = (rows, waves)
    lane = lax.broadcasted_iota(jnp.int32, shape, 1)
    wanted = lax.broadcasted_iota(jnp.int32, shape, 0) * (waves // rows)
    wanted += lax.axis_index("col")
    moments = coords_ref[...] * quad_ref[...]
    for a in range(half_steps):
        total = None
        for k in range(axes):
            line = jnp.broadcast_to(turns_ref[a, k : k + 1, :], shape)
            turn = jnp.sum(jnp.where(lane == wanted, line, 0.0), axis=1, keepdims=True)
            term = turn * moments[k : k + 1, :]
            total = term if total is None else total + term
        total = -0.5 * total if a % 2 == 0 else total
        weights_ref[a, :rows] = total
        weights_ref[a, rows:] = -total


def node_weights(coords, quad, turns, row_count):
    return pl.pallas_call(
        weights_kernel,
        out_shape=jax.ShapeDtypeStruct(
            (turns.shape[0], 2 * row_count, coords.shape[1]), coords.dtype
        ),
        compiler_params=pltpu.CompilerParams(vmem_limit_bytes=16 << 20),
    )(coords, quad, turns)


def gather_kernel(arrived_ref, final_ref):
    total = jnp.sum(arrived_ref[...].astype(jnp.float32), axis=0)
    for part in range(final_ref.shape[0]):
        final_ref[part] = total[:, part, :].astype(final_ref.dtype)


def gathered(arrived):
    _, waves_here, parts, width = arrived.shape
    return pl.pallas_call(
        gather_kernel,
        out_shape=jax.ShapeDtypeStruct((parts, waves_here, width), arrived.dtype),
        compiler_params=pltpu.CompilerParams(vmem_limit_bytes=8 << 20),
    )(arrived)


def on_device(mode_basis, node_coords, quad_weights, magnetization, decay_rates, directions):
    row_count = lax.axis_size("row")
    col_count = lax.axis_size("col")
    row_index = lax.axis_index("row")
    col_index = lax.axis_index("col")
    core = row_index % 2
    mode_count = mode_basis.shape[1]
    node_local = mode_basis.shape[0]
    parts, col_width, own_waves = magnetization.shape
    columns = 2 * row_count
    width = mode_count // 2
    f32, bf16 = jnp.float32, jnp.bfloat16

    def move(array, target):
        return lax.ppermute(array, "row", [(r, target(r)) for r in range(row_count)])

    def to_other_core(array):
        return move(array, lambda r: r ^ 1)

    def along_y(array):
        return move(array, lambda r: r ^ 8)

    def along_z(array, hops):
        return move(array, lambda r: r ^ (2 * hops))

    def over_chips(total, beside=None):
        arrived = along_y(total.astype(bf16))
        if beside is not None:
            arrived, _ = lax.optimization_barrier((arrived, beside))
        total = total + arrived.astype(f32)
        sent = total.astype(bf16)
        for hops in (1, 3, 2):
            total = total + along_z(sent, hops).astype(f32)
        return total

    waves = jnp.transpose(magnetization, (0, 2, 1))
    own_from, other_from = (core * width).reshape(1), ((1 - core) * width).reshape(1)
    first_core, first_chip = core == 0, row_index < 2
    waves, own_from, other_from, first_core, first_chip = lax.optimization_barrier(
        (waves, own_from, other_from, first_core, first_chip)
    )
    sent = spread(waves, row_count)
    sent = sent.reshape(row_count * col_count, parts, col_width)
    def half_of(array, which, axis):
        starts = [jnp.int32(0)] * array.ndim
        sizes = list(array.shape)
        starts[axis], sizes[axis] = which * width, width
        return lax.dynamic_slice_p.bind(array, *starts, slice_sizes=tuple(sizes))

    every = lax.all_to_all(sent, ("row", "col"), 0, 0)
    every = every.reshape(row_count, col_count, parts, col_width)
    every = jnp.transpose(every, (2, 0, 1, 3)).reshape(columns, mode_count)
    every, coords, quad, turns, decay_rates = lax.optimization_barrier(
        (every, node_coords, quad_weights[None, :], directions, decay_rates)
    )
    weights = node_weights(coords, quad, turns, row_count)

    def mixed(nodes, half_step):
        return lax.optimization_barrier((nodes * lax.index_in_dim(weights, half_step, 0, False)).astype(bf16))

    def swapped(array):
        rows = array.shape[0] // 2
        return lax.optimization_barrier(jnp.concatenate([array[rows:], array[:rows]], axis=0))

    rates = half_of(decay_rates, core, 0)[None, :]
    field = lax.optimization_barrier(half_of(every, core, 1))
    basis_own, basis_other = half_of(mode_basis, core, 1), half_of(mode_basis, 1 - core, 1)

    kept = lax.optimization_barrier(product(field, basis_own, NT))
    nodes = mixed(kept + product(half_of(every, 1 - core, 1), basis_other, NT), 0)
    sent = product(nodes, basis_other, NN).astype(bf16)
    kept = lax.optimization_barrier(product(nodes, basis_own, NN))
    total, own_from, other_from = lax.optimization_barrier(
        (kept + to_other_core(sent).astype(f32), own_from, other_from)
    )
    turned_own, turned_other = turned(mode_basis, own_from), turned(mode_basis, other_from)
    sums = over_chips(total, turned_own)

    def weighted(own, other, half_step):
        kept = lax.optimization_barrier(product(own, turned_own, NN))
        return mixed(kept + product(other, turned_other, NN), half_step)

    def summed(nodes):
        arrived = to_other_core(product(nodes, basis_other, NN).astype(bf16))
        kept = lax.optimization_barrier(product(nodes, basis_own, NN))
        return over_chips(kept + arrived.astype(f32))

    for step in range(STEPS):
        if step > 0:
            sums = summed(weighted(field, to_other_core(field), 2 * step))
        half = (sums + (1.0 - 0.5 * rates) * swapped(field).astype(f32)).astype(bf16)
        nodes = weighted(half, to_other_core(half), 2 * step + 1)
        if step + 1 < STEPS:
            update = summed(nodes) + (0.0 - 1.0 * rates) * swapped(half).astype(f32)
            field = (field.astype(f32) + update).astype(bf16)

    local = field.astype(f32) + (0.0 - 1.0 * rates) * swapped(half).astype(f32)
    local = jnp.where(first_chip, local, 0.0)
    part_own = (product(nodes, basis_own, NN) + local).astype(bf16)
    part_other = product(nodes, basis_other, NN).astype(bf16)
    low = jnp.where(first_core, part_own, part_other)
    high = jnp.where(first_core, part_other, part_own)
    sent = jnp.concatenate([low, high], axis=1)
    sent = sent.reshape(parts, row_count, col_count, col_width)
    sent = jnp.transpose(sent, (1, 2, 0, 3)).reshape(row_count * col_count, parts, col_width)
    every = lax.all_to_all(sent, ("row", "col"), 0, 0)
    every = every.reshape(row_count, col_count, parts, col_width)
    return jnp.transpose(gathered(every), (0, 2, 1))


def solution(mesh):
    return jax.shard_map(
        on_device,
        mesh=mesh,
        in_specs=(P("row", None), P(None, "row"), P("row"), P(None, "col", "row"), P(), P()),
        out_specs=P(None, "col", "row"),
        check_vma=False,
    )
```
